128 devices in a mesh: seq: 16 (over x, y), grp: 8 (over z, core).
Axes of the slice: x: 4, y: 4, z: 4, core: 2. Of those that a mesh axis runs over, the one named last changes fastest.
Arguments:
- tokens: bfloat16 [8, 16384, 3072], P('grp', 'seq'), may hold values from -24 to 24
- block_map: int32 [8, 128], P('grp', 'seq'), may hold values from 0 to 1, as said below
- slot_keys: bfloat16 [3072, 256], replicated, may hold values from -2 to 2
- gate_weight: bfloat16 [16, 3072, 4096], P('grp', None, 'seq'), may hold values from -0.109375 to 0.109375
- up_weight: bfloat16 [16, 3072, 4096], P('grp', None, 'seq'), may hold values from -0.109375 to 0.109375
- down_weight: bfloat16 [16, 4096, 3072], P('grp', 'seq'), may hold values from -0.09375 to 0.09375
Outputs:
- mixed: bfloat16 [8, 16384, 3072], P('grp', 'seq')
The draws below stay inside these ranges and needn't reach their ends.
Inputs may be any that keep to these rules, and one draw needn't show every extreme that they name: `block_map`: every sequence has at least one image block and at least one text block.
All inputs are finite; a program needn't handle non-finite values.
Results may differ from the reference program's by a relative error of at most 0.014.
Values may be sent and summed in bfloat16 or wider, within the bound.
A program may use at most 128 MiB of HBM per device.

```python
import math
import jax
import jax.numpy as jnp
from jax import lax

D = 3072
FF = 4096
SPE = 16
BLOCK = 128
SEQS = 8
SEQ_LEN = 16384
EXPERTS = 16
SLOTS = 256
IMG_SLOTS = 192
NBLK = 128


def slot_table(key):
    values = jax.random.normal(jax.random.fold_in(key, 11), (D, SLOTS), jnp.float32)
    return jnp.clip(values, -4.0, 4.0) * (3.0 / math.sqrt(D))


def draw_slot_keys(key, part):
    return slot_table(key).astype(jnp.bfloat16)


def draw_tokens(key, part):
    base_key = jax.random.fold_in(key, 12)
    base = jnp.clip(jax.random.normal(base_key, (SEQS, SEQ_LEN, D), jnp.float32), -6.0, 6.0)
    return base.astype(jnp.bfloat16)


def draw_block_map(key, part):
    keys = jax.random.split(jax.random.fold_in(key, 21), 4)
    thresh = jax.random.randint(keys[0], (SEQS, 1), 1, 8)
    bits = (jax.random.randint(keys[1], (SEQS, NBLK), 0, 8) < thresh).astype(jnp.int32)
    first_pos = jax.random.randint(keys[2], (SEQS,), 0, NBLK)
    second_pos = (first_pos + 1 + jax.random.randint(keys[3], (SEQS,), 0, NBLK - 1)) % NBLK
    seq_index = jnp.arange(SEQS)
    bits = bits.at[seq_index, first_pos].set(0)
    bits = bits.at[seq_index, second_pos].set(1)
    return bits.astype(jnp.int32)


def levels(key, dims, shards, least, top_value):
    gain = 1.0
    for dim, shards_of in shards:
        steps = jax.random.uniform(jax.random.fold_in(jax.random.fold_in(key, 6), dim), (shards_of,), jnp.float32, least / len(shards), top_value / len(shards))
        gain = gain * jnp.repeat(jnp.exp(steps), dims[dim] // shards_of).reshape((-1,) + (1,) * (len(dims) - 1 - dim))
    return gain


def bell_draw(key, dims, deviation, reach, cuts=(), held_as=jnp.bfloat16):
    drawn = jax.random.normal(key, dims, jnp.float32) * deviation
    if len(cuts) > 0:
        drawn = levels(key, dims, cuts, -0.22, 0.18) * drawn
    return jnp.clip(drawn, min=-reach, max=reach).astype(held_as)


def setup_inputs(seed: int = 0) -> dict:
    splits = jax.random.split(jax.random.key(seed), 7)
    tokens = draw_tokens(jax.random.fold_in(splits[6], 71), 0)
    block_map = draw_block_map(jax.random.fold_in(splits[6], 71), 0)
    slot_keys = draw_slot_keys(jax.random.fold_in(splits[6], 71), 0)
    gate_weight = bell_draw(splits[3], (EXPERTS, D, FF), D ** -0.5, 0.109375, ((0, 8), (2, 16)))
    up_weight = bell_draw(splits[4], (EXPERTS, D, FF), D ** -0.5, 0.109375, ((0, 8), (2, 16)))
    down_weight = bell_draw(splits[5], (EXPERTS, FF, D), FF ** -0.5, 0.09375, ((0, 8), (1, 16)))
    return dict(tokens=tokens, block_map=block_map, slot_keys=slot_keys, gate_weight=gate_weight, up_weight=up_weight, down_weight=down_weight)


def allowed_table(seq_map):
    slot_text = (jnp.arange(SLOTS) >= IMG_SLOTS).astype(jnp.int32)
    token_mode = jnp.repeat(seq_map, BLOCK)
    return token_mode[:, None] == slot_text[None, :]

def reference(tokens, block_map, slot_keys, gate_weight, up_weight, down_weight):

    def slot_inputs(inputs):
        seq_tokens, seq_map = inputs
        allowed = allowed_table(seq_map)
        logits = jnp.dot(seq_tokens.astype(jnp.float32), slot_keys.astype(jnp.float32), preferred_element_type=jnp.float32)
        masked = jnp.where(allowed, logits, -1e+30)
        peak_value = jnp.max(masked, axis=0)
        weights = jnp.where(allowed, jnp.exp(masked - peak_value[None, :]), 0.0)
        totals = jnp.sum(weights, axis=0)
        slot_rows = jnp.dot(weights.astype(jnp.bfloat16).T.astype(jnp.float32), seq_tokens.astype(jnp.float32), preferred_element_type=jnp.float32)
        return (slot_rows / totals[:, None]).astype(jnp.bfloat16)
    slot_in = lax.map(slot_inputs, (tokens, block_map))
    by_expert = slot_in.reshape(SEQS, EXPERTS, SPE, D).transpose(1, 0, 2, 3).reshape(EXPERTS, SEQS * SPE, D)

    def expert(inputs):
        rows_in, w_gate, w_up, w_down = inputs
        gate_sum = jnp.dot(rows_in.astype(jnp.float32), w_gate.astype(jnp.float32), preferred_element_type=jnp.float32)
        up_sum = jnp.dot(rows_in.astype(jnp.float32), w_up.astype(jnp.float32), preferred_element_type=jnp.float32)
        hidden = (jax.nn.silu(gate_sum) * up_sum).astype(jnp.bfloat16)
        return jnp.dot(hidden.astype(jnp.float32), w_down.astype(jnp.float32), preferred_element_type=jnp.float32).astype(jnp.bfloat16)
    slot_out = lax.map(expert, (by_expert, gate_weight, up_weight, down_weight))
    slot_out = slot_out.reshape(EXPERTS, SEQS, SPE, D).transpose(1, 0, 2, 3).reshape(SEQS, SLOTS, D)

    def combine(inputs):
        seq_tokens, seq_map, seq_out = inputs
        allowed = allowed_table(seq_map)
        logits = jnp.dot(seq_tokens.astype(jnp.float32), slot_keys.astype(jnp.float32), preferred_element_type=jnp.float32)
        masked = jnp.where(allowed, logits, -1e+30)
        row_peak = jnp.max(masked, axis=1)
        scores = jnp.where(allowed, jnp.exp(masked - row_peak[:, None]), 0.0)
        mix_weights = (scores / jnp.sum(scores, axis=1)[:, None]).astype(jnp.bfloat16)
        return jnp.dot(mix_weights.astype(jnp.float32), seq_out.astype(jnp.float32), preferred_element_type=jnp.float32).astype(jnp.bfloat16)
    return lax.map(combine, (tokens, block_map, slot_out))
```

```python
import functools
import jax
import jax.numpy as jnp
from jax import lax
from jax.experimental import pallas as pl
from jax.experimental.pallas import tpu as pltpu
from jax.sharding import PartitionSpec as P

BLOCK = 128
MESH = pl.DeviceIdType.MESH
F32 = jnp.float32
BF16 = jnp.bfloat16


def loop(start, stop, fn):
    def step(k, carry):
        fn(k)
        return carry

    lax.fori_loop(start, stop, step, 0)


def layer_kernel(
    dims,
    tok_hbm,
    bm_ref,
    keys_hbm,
    wg_hbm,
    wu_hbm,
    wd_hbm,
    mix_hbm,
    slots_hbm,
    tok,
    keys,
    wg,
    wu,
    wd,
    logits,
    wts,
    mixb,
    rows_f,
    fac,
    stat,
    sbuf_a,
    rbuf_a,
    part_b,
    recv_b,
    xin,
    sbuf_e,
    rbuf_e,
    part_f,
    recv_f,
    acc,
    tok_sem,
    in_sem,
    mix_sem,
    own_sem,
    st_s,
    st_r,
    a_s,
    a_r,
    b_s,
    b_r,
    c_s,
    c_r,
    e_s,
    e_r,
    f_s,
    f_r,
    g_s,
    g_r,
):
    nseq, ngrp, image_slots = dims
    me = lax.axis_index("seq")
    grp = lax.axis_index("grp")
    rows, width = tok.shape
    slots = keys.shape[1]
    cblocks = nseq // 2
    cw = width // cblocks
    half = me // cblocks
    col = pl.multiple_of(lax.rem(me, cblocks) * cw, cw)

    tchunk = rows // 4
    keys_copy = pltpu.make_async_copy(keys_hbm, keys, in_sem.at[0])
    keys_copy.start()

    def tok_copy(r):
        at = pl.ds(pl.multiple_of(r * tchunk, tchunk), tchunk)
        return pltpu.make_async_copy(tok_hbm.at[0, at], tok.at[at], tok_sem.at[r])

    loop(0, 4, lambda r: tok_copy(r).start())
    wg_copy = pltpu.make_async_copy(wg_hbm, wg, in_sem.at[1])
    wu_copy = pltpu.make_async_copy(wu_hbm, wu, in_sem.at[2])
    wd_copy = pltpu.make_async_copy(wd_hbm, wd, in_sem.at[3])
    wg_copy.start()
    wu_copy.start()
    wd_copy.start()

    barrier = pltpu.get_barrier_semaphore()

    def greet(axis, n, mine):
        def go(k):
            pl.semaphore_signal(
                barrier, inc=1, device_id={axis: lax.rem(mine + k, n)}, device_id_type=MESH
            )

        loop(1, n, go)

    greet("seq", nseq, me)
    greet("grp", ngrp, grp)

    def to(src, dst, ssem, rsem, axis, peer):
        return pltpu.make_async_remote_copy(
            src_ref=src,
            dst_ref=dst,
            send_sem=ssem,
            recv_sem=rsem,
            device_id={axis: peer},
            device_id_type=MESH,
        )

    text_lane = (lax.broadcasted_iota(jnp.int32, (1, slots), 1) >= image_slots).astype(jnp.int32)

    keys_copy.wait()

    per = tchunk // BLOCK

    def logit_chunk(r, peak):
        tok_copy(r).wait()
        at = pl.ds(pl.multiple_of(r * tchunk, tchunk), tchunk)
        got = jnp.dot(tok[at], keys[...], preferred_element_type=F32)
        for b in range(per):
            block = jnp.where(
                text_lane == bm_ref[0, r * per + b], got[b * BLOCK : (b + 1) * BLOCK], -1e30
            )
            logits[pl.ds(pl.multiple_of(r * tchunk + b * BLOCK, BLOCK), BLOCK)] = block
            peak = jnp.maximum(peak, jnp.max(block, axis=0, keepdims=True))
        return peak

    peak = lax.fori_loop(0, 4, logit_chunk, jnp.full((1, slots), -1e30, F32))

    def weigh(b, total):
        at = pl.ds(pl.multiple_of(b * BLOCK, BLOCK), BLOCK)
        w = jnp.where(text_lane == bm_ref[0, b], jnp.exp(logits[at] - peak), 0.0)
        wts[:, at] = w.T.astype(BF16)
        return total + jnp.sum(w, axis=0, keepdims=True)

    total = lax.fori_loop(0, rows // BLOCK, weigh, jnp.zeros((1, slots), F32))
    stat[me, 0:1] = peak
    stat[me, 1:2] = total

    pl.semaphore_wait(barrier, nseq - 1 + ngrp - 1)

    def stat_copy(k, peer, src):
        return to(stat.at[src], stat.at[src], st_s.at[k], st_r.at[src], "seq", peer)

    loop(1, nseq, lambda k: stat_copy(k, lax.rem(me + k, nseq), me).start())

    rw = 2 * cw

    def rows_block(n):
        at = pl.ds(pl.multiple_of(n * rw, rw), rw)
        rows_f[:, at] = jnp.dot(wts[...], tok[:, at], preferred_element_type=F32)

    loop(0, width // rw, rows_block)

    def stat_done(k):
        p = lax.rem(me + nseq - k, nseq)
        stat_copy(k, p, p).wait_recv()

    loop(1, nseq, stat_done)
    peaks = stat[:, 0, :]
    top = jnp.max(peaks, axis=0, keepdims=True)
    whole = jnp.sum(jnp.exp(peaks - top) * stat[:, 1, :], axis=0, keepdims=True)
    fac_row = jnp.exp(peak - top) / whole
    fac[...] = jnp.broadcast_to(fac_row, (BLOCK, slots)).T

    per_expert = 16
    groups = slots // (2 * per_expert)

    def scatter_a(k):
        d = lax.rem(me + k, nseq)
        h = d // cblocks
        at = pl.ds(pl.multiple_of(lax.rem(d, cblocks) * cw, cw), cw)
        for g in range(groups):
            src = pl.ds(pl.multiple_of((2 * g + h) * per_expert, per_expert), per_expert)
            scale = fac[src]
            scale = jnp.concatenate([scale] * (cw // BLOCK), axis=1)
            sbuf_a[d, g * per_expert : (g + 1) * per_expert] = (rows_f[src, at] * scale).astype(
                BF16
            )

    def a_copy(k, d, src):
        return to(sbuf_a.at[d], rbuf_a.at[src], a_s.at[k], a_r.at[src], "seq", d)

    def send_a(k):
        scatter_a(k)
        a_copy(k, lax.rem(me + k, nseq), me).start()

    loop(1, nseq, send_a)
    scatter_a(0)

    def mix_block(b):
        at = pl.ds(pl.multiple_of(b * BLOCK, BLOCK), BLOCK)
        m = logits[at]
        e = jnp.where(
            text_lane == bm_ref[0, b], jnp.exp(m - jnp.max(m, axis=1, keepdims=True)), 0.0
        )
        mixb[at] = (e / jnp.sum(e, axis=1, keepdims=True)).astype(BF16)

    loop(0, rows // BLOCK, mix_block)
    mix_copy = pltpu.make_async_copy(mixb, mix_hbm, mix_sem)
    mix_copy.start()

    acc[...] = sbuf_a[me].astype(F32)

    def gather_a(k):
        p = lax.rem(me + nseq - k, nseq)
        a_copy(k, p, p).wait_recv()
        acc[...] += rbuf_a[p].astype(F32)

    loop(1, nseq, gather_a)
    part_b[...] = acc[...].astype(BF16).reshape(part_b.shape)

    def b_copy(k, d, src):
        return to(part_b.at[d], recv_b.at[src], b_s.at[k], b_r.at[src], "grp", d)

    loop(1, ngrp, lambda k: b_copy(k, lax.rem(grp + k, ngrp), grp).start())
    recv_b[grp] = part_b[grp]

    def b_done(k):
        p = lax.rem(grp + ngrp - k, ngrp)
        b_copy(k, p, p).wait_recv()

    loop(1, ngrp, b_done)

    def c_copy(k, d, h, at, src):
        return to(recv_b, xin.at[h, :, :, at], c_s.at[k], c_r.at[src], "seq", d)

    loop(1, nseq, lambda k: c_copy(k, lax.rem(me + k, nseq), half, pl.ds(col, cw), me).start())
    xin[half, :, :, pl.ds(col, cw)] = recv_b[...]

    def c_done(k):
        p = lax.rem(me + nseq - k, nseq)
        at = pl.ds(pl.multiple_of(lax.rem(p, cblocks) * cw, cw), cw)
        c_copy(k, p, p // cblocks, at, p).wait_recv()

    loop(1, nseq, c_done)
    wg_copy.wait()
    wu_copy.wait()
    wd_copy.wait()

    lanes = ngrp * per_expert

    def expert(h):
        x = xin[h].reshape(lanes, width)
        gate = jnp.dot(x, wg[h], preferred_element_type=F32)
        up = jnp.dot(x, wu[h], preferred_element_type=F32)
        hidden = (gate / (1.0 + jnp.exp(-gate)) * up).astype(BF16)

        def down(c):
            at = pl.ds(pl.multiple_of(c * rw, rw), rw)
            out = jnp.dot(hidden, wd[h, :, at], preferred_element_type=F32).astype(BF16)
            sbuf_e[h * cblocks + 2 * c] = out[:, :cw]
            sbuf_e[h * cblocks + 2 * c + 1] = out[:, cw:]

        loop(0, cblocks // 2, down)

    loop(0, 2, expert)

    def e_copy(k, d, src):
        return to(sbuf_e.at[d], rbuf_e.at[src], e_s.at[k], e_r.at[src], "seq", d)

    loop(1, nseq, lambda k: e_copy(k, lax.rem(me + k, nseq), me).start())
    acc[...] = sbuf_e[me].astype(F32)

    def gather_e(k):
        p = lax.rem(me + nseq - k, nseq)
        e_copy(k, p, p).wait_recv()
        acc[...] += rbuf_e[p].astype(F32)

    loop(1, nseq, gather_e)
    part_f[...] = acc[...].astype(BF16).reshape(part_f.shape)

    def f_copy(k, d, src):
        return to(part_f.at[d], recv_f.at[src], f_s.at[k], f_r.at[src], "grp", d)

    loop(1, ngrp, lambda k: f_copy(k, lax.rem(grp + k, ngrp), grp).start())
    recv_f[grp] = part_f[grp]

    def f_done(k):
        p = lax.rem(grp + ngrp - k, ngrp)
        f_copy(k, p, p).wait_recv()

    loop(1, ngrp, f_done)

    def g_copy(k, d, h, at, src):
        return to(recv_f, slots_hbm.at[:, h, :, at], g_s.at[k], g_r.at[src], "seq", d)

    loop(1, nseq, lambda k: g_copy(k, lax.rem(me + k, nseq), half, pl.ds(col, cw), me).start())
    own = pltpu.make_async_copy(recv_f, slots_hbm.at[:, half, :, pl.ds(col, cw)], own_sem)
    own.start()

    def g_done(k):
        p = lax.rem(me + nseq - k, nseq)
        at = pl.ds(pl.multiple_of(lax.rem(p, cblocks) * cw, cw), cw)
        g_copy(k, p, p // cblocks, at, p).wait_recv()

    loop(1, nseq, g_done)
    own.wait()
    mix_copy.wait()

    def sent(k):
        d = lax.rem(me + k, nseq)
        stat_copy(k, d, me).wait_send()
        a_copy(k, d, me).wait_send()
        c_copy(k, d, half, pl.ds(col, cw), me).wait_send()
        e_copy(k, d, me).wait_send()
        g_copy(k, d, half, pl.ds(col, cw), me).wait_send()

    loop(1, nseq, sent)

    def sent_grp(k):
        d = lax.rem(grp + k, ngrp)
        b_copy(k, d, grp).wait_send()
        f_copy(k, d, grp).wait_send()

    loop(1, ngrp, sent_grp)


def mix_kernel(mix_ref, slots_ref, out_ref):
    for n in range(out_ref.shape[1] // 768):
        at = slice(n * 768, (n + 1) * 768)
        out_ref[:, at] = jnp.dot(
            mix_ref[...], slots_ref[:, at], preferred_element_type=F32
        ).astype(BF16)


def body(tokens, block_map, slot_keys, gate_weight, up_weight, down_weight):
    _, rows, width = tokens.shape
    slots = slot_keys.shape[1]
    nseq = lax.axis_size("seq")
    ngrp = lax.axis_size("grp")
    cw = width // (nseq // 2)
    per_expert = slots // (2 * ngrp)
    part = (ngrp, per_expert, cw)
    flat = (nseq, ngrp * per_expert, cw)
    anywhere = pl.BlockSpec(memory_space=pl.ANY)
    mix, seq_slots = pl.pallas_call(
        functools.partial(layer_kernel, (nseq, ngrp, 3 * slots // 4)),
        out_shape=(
            jax.ShapeDtypeStruct((rows, slots), BF16),
            jax.ShapeDtypeStruct((ngrp, 2, per_expert, width), BF16),
        ),
        in_specs=[anywhere, pl.BlockSpec(memory_space=pltpu.SMEM)] + [anywhere] * 4,
        out_specs=(anywhere, anywhere),
        scratch_shapes=[
            pltpu.VMEM((rows, width), BF16),
            pltpu.VMEM(slot_keys.shape, BF16),
            pltpu.VMEM(gate_weight.shape, BF16),
            pltpu.VMEM(up_weight.shape, BF16),
            pltpu.VMEM(down_weight.shape, BF16),
            pltpu.VMEM((rows, slots), F32),
            pltpu.VMEM((slots, rows), BF16),
            pltpu.VMEM((rows, slots), BF16),
            pltpu.VMEM((slots, width), F32),
            pltpu.VMEM((slots, BLOCK), F32),
            pltpu.VMEM((nseq, 2, slots), F32),
            pltpu.VMEM(flat, BF16),
            pltpu.VMEM(flat, BF16),
            pltpu.VMEM(part, BF16),
            pltpu.VMEM(part, BF16),
            pltpu.VMEM((2, ngrp, per_expert, width), BF16),
            pltpu.VMEM(flat, BF16),
            pltpu.VMEM(flat, BF16),
            pltpu.VMEM(part, BF16),
            pltpu.VMEM(part, BF16),
            pltpu.VMEM(flat[1:], F32),
            pltpu.SemaphoreType.DMA((4,)),
            pltpu.SemaphoreType.DMA((4,)),
            pltpu.SemaphoreType.DMA,
            pltpu.SemaphoreType.DMA,
        ]
        + [
            pltpu.SemaphoreType.DMA((n,))
            for n in (nseq, nseq, nseq, nseq, ngrp, ngrp, nseq, nseq)
            + (nseq, nseq, ngrp, ngrp, nseq, nseq)
        ],
        compiler_params=pltpu.CompilerParams(
            collective_id=0, has_side_effects=True, vmem_limit_bytes=52 << 20
        ),
    )(tokens, block_map, slot_keys, gate_weight, up_weight, down_weight)

    tile = rows // 4
    out = pl.pallas_call(
        mix_kernel,
        grid=(4,),
        out_shape=jax.ShapeDtypeStruct((rows, width), BF16),
        in_specs=[
            pl.BlockSpec((tile, slots), lambda i: (i, 0)),
            pl.BlockSpec((slots, width), lambda i: (0, 0)),
        ],
        out_specs=pl.BlockSpec((tile, width), lambda i: (i, 0)),
        compiler_params=pltpu.CompilerParams(vmem_limit_bytes=24 << 20),
    )(mix, seq_slots.reshape(slots, width))
    return out[None]


def solution(mesh):
    placed = (
        P("grp", "seq", None),
        P("grp", "seq"),
        P(),
        P("grp", None, "seq"),
        P("grp", None, "seq"),
        P("grp", "seq", None),
    )
    return jax.shard_map(
        body, mesh=mesh, in_specs=placed, out_specs=P("grp", "seq", None), check_vma=False
    )
```

```python
import functools
import jax
import jax.numpy as jnp
from jax import lax
from jax.experimental import pallas as pl
from jax.experimental.pallas import tpu as pltpu
from jax.sharding import PartitionSpec as P

BLOCK = 128
SIDE = 4
CHUNKS = 3
MESH = pl.DeviceIdType.MESH
F32 = jnp.float32
BF16 = jnp.bfloat16


def loop(start, stop, fn):
    def step(k, carry):
        fn(k)
        return carry

    lax.fori_loop(start, stop, step, 0)


def layer_kernel(
    dims,
    tok_hbm,
    bm_hbm,
    keys_hbm,
    wg_hbm,
    wu_hbm,
    wd_hbm,
    mix_hbm,
    slots_hbm,
    tok,
    bm,
    keys,
    wg,
    wu,
    wd,
    logits,
    wts,
    mixb,
    fac,
    stat,
    terms,
    first,
    middle,
    second,
    grp_out,
    grp_in,
    xs,
    gates,
    ups,
    ys,
    tok_sem,
    in_sem,
    mix_sem,
    own_sem,
    stat_s,
    stat_r,
    sum_hs,
    sum_hr,
    sum_ls,
    sum_lr,
    grp_s,
    grp_r,
    put_ls,
    put_lr,
    put_hs,
    put_hr,
):
    nseq, ngrp, image_slots = dims
    me = lax.axis_index("seq")
    grp = lax.axis_index("grp")
    rows, width = tok.shape
    slots = keys.shape[1]
    tchunk = rows // 4
    blocks = rows // BLOCK
    cw = width // CHUNKS
    bw = cw // 2
    pw = bw // SIDE
    prow = slots // 4
    at_x, at_y = me // SIDE, lax.rem(me, SIDE)
    place = ((at_x, at_y), (at_y, at_x))

    def seq_of(h, u, v):
        return u * SIDE + v if h == 0 else v * SIDE + u

    def block_cols(s, u):
        return pl.ds(pl.multiple_of(s * cw + lax.rem(u, 2) * bw, bw), bw)

    def piece_cols(s, u, v):
        return pl.ds(pl.multiple_of(s * cw + lax.rem(u, 2) * bw + v * pw, pw), pw)

    def piece_at(v):
        return pl.ds(pl.multiple_of(v * pw, pw), pw)

    bm_copy = pltpu.make_async_copy(bm_hbm, bm, in_sem.at[4])
    bm_copy.start()
    keys_copy = pltpu.make_async_copy(keys_hbm, keys, in_sem.at[0])
    keys_copy.start()

    def tok_copy(r):
        at = pl.ds(pl.multiple_of(r * tchunk, tchunk), tchunk)
        return pltpu.make_async_copy(tok_hbm.at[0, at], tok.at[at], tok_sem.at[r])

    loop(0, 4, lambda r: tok_copy(r).start())
    wg_copy = pltpu.make_async_copy(wg_hbm, wg, in_sem.at[1])
    wu_copy = pltpu.make_async_copy(wu_hbm, wu, in_sem.at[2])
    wd_copy = pltpu.make_async_copy(wd_hbm, wd, in_sem.at[3])

    barrier = pltpu.get_barrier_semaphore()

    def greet(axis, n, mine):
        def go(k):
            pl.semaphore_signal(
                barrier, inc=1, device_id={axis: lax.rem(mine + k, n)}, device_id_type=MESH
            )

        loop(1, n, go)

    greet("seq", nseq, me)
    greet("grp", ngrp, grp)

    def to(src, dst, ssem, rsem, axis, peer):
        return pltpu.make_async_remote_copy(
            src_ref=src,
            dst_ref=dst,
            send_sem=ssem,
            recv_sem=rsem,
            device_id={axis: peer},
            device_id_type=MESH,
        )

    text_lane = (lax.broadcasted_iota(jnp.int32, (1, slots), 1) >= image_slots).astype(jnp.int32)

    def by_stream(x):
        wide = slots // 16
        return jnp.concatenate(
            [
                x[(2 * g + h) * 16 + t * 8 : (2 * g + h) * 16 + t * 8 + 8]
                for h in range(2)
                for t in range(2)
                for g in range(wide // 2)
            ],
            axis=0,
        )

    bm_copy.wait()
    keys_copy.wait()
    per = tchunk // BLOCK

    def logit_chunk(r, peak):
        tok_copy(r).wait()
        at = pl.ds(pl.multiple_of(r * tchunk, tchunk), tchunk)
        got = jnp.dot(tok[at], keys[...], preferred_element_type=F32)
        for b in range(per):
            block = jnp.where(
                text_lane == bm[0, r * per + b], got[b * BLOCK : (b + 1) * BLOCK], -1e30
            )
            logits[pl.ds(pl.multiple_of(r * tchunk + b * BLOCK, BLOCK), BLOCK)] = block
            peak = jnp.maximum(peak, jnp.max(block, axis=0, keepdims=True))
        return peak

    peak = lax.fori_loop(0, 4, logit_chunk, jnp.full((1, slots), -1e30, F32))
    wg_copy.start()
    wu_copy.start()
    wd_copy.start()

    def weigh(b, total):
        at = pl.ds(pl.multiple_of(b * BLOCK, BLOCK), BLOCK)
        w = jnp.where(text_lane == bm[0, b], jnp.exp(logits[at] - peak), 0.0)
        wts[:, at] = by_stream(w.T).astype(BF16)
        return total + jnp.sum(w, axis=0, keepdims=True)

    total = lax.fori_loop(0, blocks, weigh, jnp.zeros((1, slots), F32))
    stat[me, 0:1] = peak
    stat[me, 1:2] = total

    pl.semaphore_wait(barrier, nseq - 1 + ngrp - 1)

    def stat_copy(k, peer, src):
        return to(stat.at[src], stat.at[src], stat_s.at[k], stat_r.at[src], "seq", peer)

    loop(1, nseq, lambda k: stat_copy(k, lax.rem(me + k, nseq), me).start())

    def around(n, at, k):
        return lax.rem(at + k, n)

    def before(n, at, k):
        return lax.rem(at + n - k, n)

    def sum_heavy(p, h, s, k, dst, src):
        _, v = place[h]
        return to(
            terms.at[p, h, dst // 2, :, block_cols(s, dst)],
            first.at[p, h, s, src],
            sum_hs.at[p, h, s, k],
            sum_hr.at[p, h, s, src],
            "seq",
            seq_of(h, dst, v),
        )

    def sum_light(p, h, s, k, dst, src):
        u, _ = place[h]
        return to(
            middle.at[p, h, s, :, piece_at(dst)],
            second.at[p, h, s, src],
            sum_ls.at[p, h, s, k],
            sum_lr.at[p, h, s, src],
            "seq",
            seq_of(h, u, dst),
        )

    def swap(p, h, s, k, dst, src):
        return to(
            grp_out.at[p, h, s, dst],
            grp_in.at[p, h, s, src],
            grp_s.at[p, h, s, k],
            grp_r.at[p, h, s, src],
            "grp",
            dst,
        )

    def put_light(p, h, s, k, dst, src):
        u, v = place[h]
        if p == 0:
            here = xs.at[h, u // 2, :, piece_cols(s, u, v)]
            there = xs.at[h, u // 2, :, piece_cols(s, u, src)]
        else:
            here = ys.at[h, s, :, :, piece_at(v)]
            there = ys.at[h, s, :, :, piece_at(src)]
        return to(
            here,
            there,
            put_ls.at[p, h, s, k],
            put_lr.at[p, h, s, src],
            "seq",
            seq_of(h, u, dst),
        )

    def put_heavy(p, h, s, k, dst, src):
        u, v = place[h]
        if p == 0:
            here = xs.at[h, u // 2, :, block_cols(s, u)]
            there = xs.at[h, src // 2, :, block_cols(s, src)]
        else:
            here = ys.at[h, s]
            there = slots_hbm.at[:, h, src // 2, :, block_cols(s, src)]
        return to(
            here,
            there,
            put_hs.at[p, h, s, k],
            put_hr.at[p, h, s, src],
            "seq",
            seq_of(h, dst, v),
        )

    def own_copy(h, s):
        u, _ = place[h]
        return pltpu.make_async_copy(
            ys.at[h, s], slots_hbm.at[:, h, u // 2, :, block_cols(s, u)], own_sem.at[h, s]
        )

    def start_sum(p, h, s):
        u, _ = place[h]
        loop(1, SIDE, lambda k: sum_heavy(p, h, s, k, around(SIDE, u, k), u).start())

    def mid_sum(p, h, s):
        u, v = place[h]
        acc = terms[p, h, u // 2, :, block_cols(s, u)].astype(F32)
        scale = [None] * SIDE
        if p == 0:
            mine = fac[pl.ds(pl.multiple_of(h * 2 * prow + (u // 2) * prow, prow), prow)]
            scale = [mine[:, h * SIDE + k : h * SIDE + k + 1] for k in range(SIDE)]
            acc = acc * scale[0]
        for k in range(1, SIDE):
            src = before(SIDE, u, k)
            sum_heavy(p, h, s, k, src, src).wait_recv()
            got = first[p, h, s, src].astype(F32)
            acc = acc + (got if p else got * scale[k])
        middle[p, h, s] = acc.astype(BF16)
        loop(1, SIDE, lambda k: sum_light(p, h, s, k, around(SIDE, v, k), v).start())

    def end_sum(p, h, s):
        _, v = place[h]
        acc = middle[p, h, s, :, piece_at(v)].astype(F32)
        for k in range(1, SIDE):
            src = before(SIDE, v, k)
            sum_light(p, h, s, k, src, src).wait_recv()
            acc = acc + second[p, h, s, src].astype(F32)
        grp_out[p, h, s] = acc.reshape(grp_out.shape[3:]).astype(BF16)
        loop(1, ngrp, lambda k: swap(p, h, s, k, around(ngrp, grp, k), grp).start())
        grp_in[p, h, s, grp] = grp_out[p, h, s, grp]

    def start_put(p, h, s):
        u, v = place[h]
        for k in range(1, ngrp):
            src = before(ngrp, grp, k)
            swap(p, h, s, k, src, src).wait_recv()
        if p == 0:
            xs[h, u // 2, :, piece_cols(s, u, v)] = grp_in[p, h, s].reshape(prow, pw)
        else:
            ys[h, s, :, :, piece_at(v)] = grp_in[p, h, s]
        loop(1, SIDE, lambda k: put_light(p, h, s, k, around(SIDE, v, k), v).start())

    def mid_put(p, h, s):
        u, v = place[h]
        for k in range(1, SIDE):
            src = before(SIDE, v, k)
            put_light(p, h, s, k, src, src).wait_recv()
        loop(1, SIDE, lambda k: put_heavy(p, h, s, k, around(SIDE, u, k), u).start())
        if p == 1:
            own_copy(h, s).start()

    def end_put(p, h, s):
        u, _ = place[h]
        for k in range(1, SIDE):
            src = before(SIDE, u, k)
            put_heavy(p, h, s, k, src, src).wait_recv()
        if p == 1:
            own_copy(h, s).wait()
            return
        x = xs[h, :, :, s * cw : (s + 1) * cw].reshape(2 * prow, cw)
        gate = jnp.dot(x, wg[h, s * cw : (s + 1) * cw], preferred_element_type=F32)
        up = jnp.dot(x, wu[h, s * cw : (s + 1) * cw], preferred_element_type=F32)
        if s > 0:
            gate = gate + gates[h]
            up = up + ups[h]
        if s < CHUNKS - 1:
            gates[h] = gate
            ups[h] = up
            return
        hidden = (gate / (1.0 + jnp.exp(-gate)) * up).astype(BF16)
        for n in range(CHUNKS):
            at = slice(n * cw, (n + 1) * cw)
            out = jnp.dot(hidden, wd[h, :, at], preferred_element_type=F32)
            terms[1, h, :, :, at] = out.reshape(2, prow, cw).astype(BF16)
            start_sum(1, h, n)

    def mix_rows(b):
        at = pl.ds(pl.multiple_of(b * BLOCK, BLOCK), BLOCK)
        m = logits[at]
        e = jnp.where(text_lane == bm[0, b], jnp.exp(m - jnp.max(m, axis=1, keepdims=True)), 0.0)
        mixb[at] = (e / jnp.sum(e, axis=1, keepdims=True)).astype(BF16)

    for s in range(CHUNKS):
        at = slice(s * cw, (s + 1) * cw)
        out = jnp.dot(wts[...], tok[:, at], preferred_element_type=F32)
        terms[0, :, :, :, at] = out.reshape(2, 2, prow, cw).astype(BF16)
        for h in range(2):
            start_sum(0, h, s)

    def stat_done(k):
        src = before(nseq, me, k)
        stat_copy(k, src, src).wait_recv()

    loop(1, nseq, stat_done)
    peaks = stat[:, 0, :]
    top = jnp.max(peaks, axis=0, keepdims=True)
    whole = jnp.sum(jnp.exp(peaks - top) * stat[:, 1, :], axis=0, keepdims=True)
    near = []
    for h in range(2):
        u, v = place[h]
        for k in range(SIDE):
            near.append(stat[seq_of(h, before(SIDE, u, k), v), 0:1])
    near = jnp.exp(jnp.concatenate(near, axis=0) - top) / whole
    fac[...] = by_stream(jnp.concatenate([near] * (BLOCK // (2 * SIDE)), axis=0).T)

    steps = (mid_sum, end_sum, start_put, mid_put, end_put)
    mix_copy = pltpu.make_async_copy(mixb, mix_hbm, mix_sem)

    for p in range(2):
        for tick in range(len(steps) + CHUNKS - 1):
            for n in reversed(range(len(steps))):
                s = tick - n
                if 0 <= s < CHUNKS:
                    for h in range(2):
                        steps[n](p, h, s)
            if p == 0 and tick == CHUNKS:
                wg_copy.wait()
                wu_copy.wait()
                wd_copy.wait()
                loop(0, blocks, mix_rows)
                mix_copy.start()

    mix_copy.wait()

    def stat_sent(k):
        stat_copy(k, around(nseq, me, k), me).wait_send()

    loop(1, nseq, stat_sent)
    for p in range(2):
        for h in range(2):
            u, v = place[h]

            def sent(s):
                for k in range(1, SIDE):
                    sum_heavy(p, h, s, k, around(SIDE, u, k), u).wait_send()
                    sum_light(p, h, s, k, around(SIDE, v, k), v).wait_send()
                    put_light(p, h, s, k, around(SIDE, v, k), v).wait_send()
                    put_heavy(p, h, s, k, around(SIDE, u, k), u).wait_send()
                for k in range(1, ngrp):
                    swap(p, h, s, k, around(ngrp, grp, k), grp).wait_send()

            loop(0, CHUNKS, sent)


def mix_kernel(mix_ref, slots_ref, out_ref):
    step = out_ref.shape[1] // CHUNKS
    for n in range(CHUNKS):
        at = slice(n * step, (n + 1) * step)
        out_ref[:, at] = jnp.dot(
            mix_ref[...], slots_ref[:, at], preferred_element_type=F32
        ).astype(BF16)


def body(tokens, block_map, slot_keys, gate_weight, up_weight, down_weight):
    _, rows, width = tokens.shape
    slots = slot_keys.shape[1]
    nseq = lax.axis_size("seq")
    ngrp = lax.axis_size("grp")
    hidden = gate_weight.shape[2]
    cw = width // CHUNKS
    bw = cw // 2
    pw = bw // SIDE
    prow = slots // 4
    per = prow // ngrp
    anywhere = pl.BlockSpec(memory_space=pl.ANY)
    streams = (2, 2, CHUNKS)
    dma = pltpu.SemaphoreType.DMA
    mix, seq_slots = pl.pallas_call(
        functools.partial(layer_kernel, (nseq, ngrp, 3 * slots // 4)),
        out_shape=(
            jax.ShapeDtypeStruct((rows, slots), BF16),
            jax.ShapeDtypeStruct((ngrp, 2, 2, per, width), BF16),
        ),
        in_specs=[anywhere] * 6,
        out_specs=(anywhere, anywhere),
        scratch_shapes=[
            pltpu.VMEM((rows, width), BF16),
            pltpu.SMEM(block_map.shape, jnp.int32),
            pltpu.VMEM(slot_keys.shape, BF16),
            pltpu.VMEM(gate_weight.shape, BF16),
            pltpu.VMEM(up_weight.shape, BF16),
            pltpu.VMEM(down_weight.shape, BF16),
            pltpu.VMEM((rows, slots), F32),
            pltpu.VMEM((slots, rows), BF16),
            pltpu.VMEM((rows, slots), BF16),
            pltpu.VMEM((slots, BLOCK), F32),
            pltpu.VMEM((nseq, 2, slots), F32),
            pltpu.VMEM((2, 2, 2, prow, width), BF16),
            pltpu.VMEM((*streams, SIDE, prow, bw), BF16),
            pltpu.VMEM((*streams, prow, bw), BF16),
            pltpu.VMEM((*streams, SIDE, prow, pw), BF16),
            pltpu.VMEM((*streams, ngrp, per, pw), BF16),
            pltpu.VMEM((*streams, ngrp, per, pw), BF16),
            pltpu.VMEM((2, 2, prow, width), BF16),
            pltpu.VMEM((2, 2 * prow, hidden), F32),
            pltpu.VMEM((2, 2 * prow, hidden), F32),
            pltpu.VMEM((2, CHUNKS, ngrp, per, bw), BF16),
            dma((4,)),
            dma((5,)),
            dma,
            dma((2, CHUNKS)),
            dma((nseq,)),
            dma((nseq,)),
            dma((*streams, SIDE)),
            dma((*streams, SIDE)),
            dma((*streams, SIDE)),
            dma((*streams, SIDE)),
            dma((*streams, ngrp)),
            dma((*streams, ngrp)),
            dma((*streams, SIDE)),
            dma((*streams, SIDE)),
            dma((*streams, SIDE)),
            dma((*streams, SIDE)),
        ],
        compiler_params=pltpu.CompilerParams(
            collective_id=0, has_side_effects=True, vmem_limit_bytes=52 << 20
        ),
    )(tokens, block_map, slot_keys, gate_weight, up_weight, down_weight)

    tile = rows // 4
    out = pl.pallas_call(
        mix_kernel,
        grid=(4,),
        out_shape=jax.ShapeDtypeStruct((rows, width), BF16),
        in_specs=[
            pl.BlockSpec((tile, slots), lambda i: (i, 0)),
            pl.BlockSpec((slots, width), lambda i: (0, 0)),
        ],
        out_specs=pl.BlockSpec((tile, width), lambda i: (i, 0)),
        compiler_params=pltpu.CompilerParams(vmem_limit_bytes=60 << 20),
    )(mix, seq_slots.reshape(slots, width))
    return out[None]


def solution(mesh):
    placed = (
        P("grp", "seq", None),
        P("grp", "seq"),
        P(),
        P("grp", None, "seq"),
        P("grp", None, "seq"),
        P("grp", "seq", None),
    )
    return jax.shard_map(
        body, mesh=mesh, in_specs=placed, out_specs=P("grp", "seq", None), check_vma=False
    )
```

```python
import functools
import jax
import jax.numpy as jnp
from jax import lax
from jax.experimental import pallas as pl
from jax.experimental.pallas import tpu as pltpu
from jax.sharding import PartitionSpec as P

BLOCK = 128
SIDE = 4
CHUNKS = 3
MESH = pl.DeviceIdType.MESH
F32 = jnp.float32
BF16 = jnp.bfloat16


def loop(start, stop, fn):
    def step(k, carry):
        fn(k)
        return carry

    lax.fori_loop(start, stop, step, 0)


def layer_kernel(
    dims,
    tok_hbm,
    bm_hbm,
    keys_hbm,
    wg_hbm,
    wu_hbm,
    wd_hbm,
    mix_hbm,
    slots_hbm,
    tok,
    bm,
    keys,
    wg,
    wu,
    wd,
    logits,
    wts,
    mixb,
    fac,
    scales,
    stat,
    terms,
    first,
    middle,
    second,
    xs,
    gates,
    ups,
    ys,
    tok_sem,
    in_sem,
    mix_sem,
    own_sem,
    sent,
    stat_r,
    sum_hr,
    sum_lr,
    put_lr,
    put_hr,
):
    nseq, ngrp, image_slots = dims
    me = lax.axis_index("seq")
    grp = lax.axis_index("grp")
    rows, width = tok.shape
    slots = keys.shape[1]
    tchunk = rows // 4
    blocks = rows // BLOCK
    cw = width // CHUNKS
    bw = cw // 2
    pw = bw // SIDE
    prow = slots // 4
    at_x, at_y = me // SIDE, lax.rem(me, SIDE)
    place = ((at_x, at_y), (at_y, at_x))

    def seq_of(h, u, v):
        return u * SIDE + v if h == 0 else v * SIDE + u

    def block_cols(s, u):
        return pl.ds(pl.multiple_of(s * cw + lax.rem(u, 2) * bw, bw), bw)

    def piece_cols(s, u, v):
        return pl.ds(pl.multiple_of(s * cw + lax.rem(u, 2) * bw + v * pw, pw), pw)

    def piece_at(v):
        return pl.ds(pl.multiple_of(v * pw, pw), pw)

    bm_copy = pltpu.make_async_copy(bm_hbm, bm, in_sem.at[4])
    bm_copy.start()
    keys_copy = pltpu.make_async_copy(keys_hbm, keys, in_sem.at[0])
    keys_copy.start()

    def tok_copy(r):
        at = pl.ds(pl.multiple_of(r * tchunk, tchunk), tchunk)
        return pltpu.make_async_copy(tok_hbm.at[0, at], tok.at[at], tok_sem.at[r])

    loop(0, 4, lambda r: tok_copy(r).start())
    wg_copy = pltpu.make_async_copy(wg_hbm, wg, in_sem.at[1])
    wu_copy = pltpu.make_async_copy(wu_hbm, wu, in_sem.at[2])
    wd_copy = pltpu.make_async_copy(wd_hbm, wd, in_sem.at[3])

    barrier = pltpu.get_barrier_semaphore()

    def greet(peer):
        pl.semaphore_signal(barrier, inc=1, device_id=peer, device_id_type=MESH)

    for h in range(2):
        u, v = place[h]

        def greet_line(k):
            peer = seq_of(h, u, lax.rem(v + k // ngrp, SIDE))
            greet({"seq": peer, "grp": lax.rem(grp + k, ngrp)})

        loop(ngrp if h else 1, SIDE * ngrp, greet_line)

    def greet_rest(k):
        x = lax.rem(at_x + 1 + k // (SIDE - 1), SIDE)
        y = lax.rem(at_y + 1 + lax.rem(k, SIDE - 1), SIDE)
        greet({"seq": x * SIDE + y})

    loop(0, (SIDE - 1) * (SIDE - 1), greet_rest)
    greeted = (2 * SIDE - 1) * ngrp - 1 + (SIDE - 1) * (SIDE - 1)

    def to(src, dst, ssem, rsem, peer, **more):
        return pltpu.make_async_remote_copy(
            src_ref=src,
            dst_ref=dst,
            send_sem=ssem,
            recv_sem=rsem,
            device_id={"seq": peer, **more},
            device_id_type=MESH,
        )

    text_lane = (lax.broadcasted_iota(jnp.int32, (1, slots), 1) >= image_slots).astype(jnp.int32)

    def by_stream(x):
        wide = slots // 16
        return jnp.concatenate(
            [
                x[(2 * g + h) * 16 + t * 8 : (2 * g + h) * 16 + t * 8 + 8]
                for h in range(2)
                for t in range(2)
                for g in range(wide // 2)
            ],
            axis=0,
        )

    bm_copy.wait()
    keys_copy.wait()
    per = tchunk // BLOCK

    def logit_chunk(r, peak):
        tok_copy(r).wait()
        at = pl.ds(pl.multiple_of(r * tchunk, tchunk), tchunk)
        got = jnp.dot(tok[at], keys[...], preferred_element_type=F32)
        for b in range(per):
            block = jnp.where(
                text_lane == bm[0, r * per + b], got[b * BLOCK : (b + 1) * BLOCK], -1e30
            )
            logits[pl.ds(pl.multiple_of(r * tchunk + b * BLOCK, BLOCK), BLOCK)] = block
            peak = jnp.maximum(peak, jnp.max(block, axis=0, keepdims=True))
        return peak

    peak = lax.fori_loop(0, 4, logit_chunk, jnp.full((1, slots), -1e30, F32))
    wg_copy.start()
    wu_copy.start()
    wd_copy.start()

    def weigh(b, total):
        at = pl.ds(pl.multiple_of(b * BLOCK, BLOCK), BLOCK)
        w = jnp.where(text_lane == bm[0, b], jnp.exp(logits[at] - peak), 0.0)
        wts[:, at] = by_stream(w.T).astype(BF16)
        return total + jnp.sum(w, axis=0, keepdims=True)

    total = lax.fori_loop(0, blocks, weigh, jnp.zeros((1, slots), F32))
    stat[me, 0:1] = peak
    stat[me, 1:2] = total

    pl.semaphore_wait(barrier, greeted)

    def stat_copy(peer, src):
        return to(stat.at[src], stat.at[src], sent.at[0, 0], stat_r, peer)

    loop(1, nseq, lambda k: stat_copy(lax.rem(me + k, nseq), me).start())

    def around(n, at, k):
        return lax.rem(at + k, n)

    def before(n, at, k):
        return lax.rem(at + n - k, n)

    def sum_heavy(p, h, s, dst, src):
        _, v = place[h]
        return to(
            terms.at[p, h, dst // 2, :, block_cols(s, dst)],
            first.at[p, h, s, src],
            sent.at[1, p],
            sum_hr.at[p, h, s],
            seq_of(h, dst, v),
        )

    def sum_light(p, h, s, dst, dst_grp, src, src_grp):
        u, _ = place[h]
        return to(
            middle.at[p, h, s, dst_grp, :, piece_at(dst)],
            second.at[p, h, s, src * ngrp + src_grp],
            sent.at[2, p],
            sum_lr.at[p, h, s],
            seq_of(h, u, dst),
            grp=dst_grp,
        )

    def put_light(p, h, s, dst, src):
        u, v = place[h]
        if p == 0:
            here = xs.at[h, u // 2, :, piece_cols(s, u, v)]
            there = xs.at[h, u // 2, :, piece_cols(s, u, src)]
        else:
            here = ys.at[h, s, :, :, piece_at(v)]
            there = ys.at[h, s, :, :, piece_at(src)]
        return to(
            here,
            there,
            sent.at[3, p],
            put_lr.at[p, h, s],
            seq_of(h, u, dst),
        )

    def put_heavy(p, h, s, dst, src):
        u, v = place[h]
        if p == 0:
            here = xs.at[h, u // 2, :, block_cols(s, u)]
            there = xs.at[h, src // 2, :, block_cols(s, src)]
        else:
            here = ys.at[h, s]
            there = slots_hbm.at[:, h, src // 2, :, block_cols(s, src)]
        return to(
            here,
            there,
            sent.at[4, p],
            put_hr.at[p, h, s],
            seq_of(h, dst, v),
        )

    def own_copy(h, s):
        u, _ = place[h]
        return pltpu.make_async_copy(
            ys.at[h, s], slots_hbm.at[:, h, u // 2, :, block_cols(s, u)], own_sem.at[h, s]
        )

    def start_sum(p, h, s):
        u, _ = place[h]
        loop(1, SIDE, lambda k: sum_heavy(p, h, s, around(SIDE, u, k), u).start())

    def arrived(ref, sem):
        pltpu.make_async_copy(ref, ref, sem).wait()

    def mid_sum(p, h, s):
        u, v = place[h]
        acc = terms[p, h, u // 2, :, block_cols(s, u)].astype(F32)
        arrived(first.at[p, h, s, : SIDE - 1], sum_hr.at[p, h, s])
        if p == 0:
            acc = acc * scale_of(h, 0)
        for k in range(1, SIDE):
            got = first[p, h, s, before(SIDE, u, k)].astype(F32)
            acc = acc + (got if p else got * scale_of(h, k))
        middle[p, h, s] = acc.reshape(middle.shape[3:]).astype(BF16)

        def send(k):
            dst, dst_grp = around(SIDE, v, k // ngrp), around(ngrp, grp, k)
            sum_light(p, h, s, dst, dst_grp, v, grp).start()

        loop(1, SIDE * ngrp, send)
        second[p, h, s, v * ngrp + grp] = middle[p, h, s, grp, :, piece_at(v)]

    def scale_of(h, k):
        return jnp.concatenate([scales[h, k]] * (bw // BLOCK), axis=1)

    def end_sum(p, h, s):
        u, v = place[h]
        arrived(second.at[p, h, s, : SIDE * ngrp - 1], sum_lr.at[p, h, s])
        acc = second[p, h, s, :ngrp].astype(F32)
        for k in range(1, SIDE):
            acc = acc + second[p, h, s, k * ngrp : (k + 1) * ngrp].astype(F32)
        if p == 0:
            piece = acc.reshape(prow, pw).astype(BF16)
            xs[h, u // 2, :, piece_cols(s, u, v)] = piece
        else:
            ys[h, s, :, :, piece_at(v)] = acc.astype(BF16)
        loop(1, SIDE, lambda k: put_light(p, h, s, around(SIDE, v, k), v).start())

    def mid_put(p, h, s):
        u, v = place[h]
        arrived(ys.at[h, s, :, :, : (SIDE - 1) * pw], put_lr.at[p, h, s])
        loop(1, SIDE, lambda k: put_heavy(p, h, s, around(SIDE, u, k), u).start())
        if p == 1:
            own_copy(h, s).start()

    def end_put(p, h, s):
        arrived(first.at[p, h, s, : SIDE - 1], put_hr.at[p, h, s])
        if p == 1:
            own_copy(h, s).wait()
            return
        x = xs[h, :, :, s * cw : (s + 1) * cw].reshape(2 * prow, cw)
        gate = jnp.dot(x, wg[h, s * cw : (s + 1) * cw], preferred_element_type=F32)
        up = jnp.dot(x, wu[h, s * cw : (s + 1) * cw], preferred_element_type=F32)
        if s > 0:
            gate = gate + gates[h]
            up = up + ups[h]
        if s < CHUNKS - 1:
            gates[h] = gate
            ups[h] = up
            return
        hidden = (gate / (1.0 + jnp.exp(-gate)) * up).astype(BF16)
        for n in range(CHUNKS):
            at = slice(n * cw, (n + 1) * cw)
            out = jnp.dot(hidden, wd[h, :, at], preferred_element_type=F32)
            terms[1, h, :, :, at] = out.reshape(2, prow, cw).astype(BF16)
            if n < CHUNKS - 1:
                start_sum(1, h, n)

    def mix_rows(b):
        at = pl.ds(pl.multiple_of(b * BLOCK, BLOCK), BLOCK)
        m = logits[at]
        e = jnp.where(text_lane == bm[0, b], jnp.exp(m - jnp.max(m, axis=1, keepdims=True)), 0.0)
        mixb[at] = (e / jnp.sum(e, axis=1, keepdims=True)).astype(BF16)

    for s in range(CHUNKS):
        at = slice(s * cw, (s + 1) * cw)
        out = jnp.dot(wts[...], tok[:, at], preferred_element_type=F32)
        terms[0, :, :, :, at] = out.reshape(2, 2, prow, cw).astype(BF16)
        if s < CHUNKS - 1:
            for h in range(2):
                start_sum(0, h, s)

    loop(0, blocks, mix_rows)
    mix_copy = pltpu.make_async_copy(mixb, mix_hbm, mix_sem)
    mix_copy.start()
    arrived(stat.at[: nseq - 1], stat_r)
    peaks = stat[:, 0, :]
    top = jnp.max(peaks, axis=0, keepdims=True)
    whole = jnp.sum(jnp.exp(peaks - top) * stat[:, 1, :], axis=0, keepdims=True)
    near = []
    for h in range(2):
        u, v = place[h]
        for k in range(SIDE):
            near.append(stat[seq_of(h, before(SIDE, u, k), v), 0:1])
    near = jnp.exp(jnp.concatenate(near, axis=0) - top) / whole
    fac[...] = by_stream(jnp.concatenate([near] * (BLOCK // (2 * SIDE)), axis=0).T)
    for h in range(2):
        u, _ = place[h]
        mine = fac[pl.ds(pl.multiple_of(h * 2 * prow + (u // 2) * prow, prow), prow)]
        for k in range(SIDE):
            scales[h, k] = jnp.broadcast_to(
                mine[:, h * SIDE + k : h * SIDE + k + 1], (prow, BLOCK)
            )

    order = (
        (mid_sum, 0),
        (start_sum, 2),
        (mid_sum, 1),
        (end_sum, 0),
        (mid_sum, 2),
        (end_sum, 1),
        (mid_put, 0),
        (end_sum, 2),
        (mid_put, 1),
        (mid_put, 2),
        (end_put, 0),
        (end_put, 1),
        (end_put, 2),
    )

    for p in range(2):
        for step, s in order:
            if p == 0 and (step, s) == (end_put, 0):
                wg_copy.wait()
                wu_copy.wait()
                wd_copy.wait()
            for h in range(2):
                step(p, h, s)

    mix_copy.wait()

    arrived(stat.at[: nseq - 1], sent.at[0, 0])
    for p in range(2):
        arrived(first.at[p, :, :, : SIDE - 1], sent.at[1, p])
        arrived(second.at[p, :, :, : SIDE * ngrp - 1], sent.at[2, p])
        arrived(ys.at[:, :, :, :, : (SIDE - 1) * pw], sent.at[3, p])
        arrived(first.at[p, :, :, : SIDE - 1], sent.at[4, p])


def mix_kernel(mix_hbm, slots_hbm, out_hbm, mix, slots, out, mix_sem, in_sem, out_sem):
    parts, slot_count, tile = slots.shape
    mix_copy = pltpu.make_async_copy(mix_hbm, mix, mix_sem)
    mix_copy.start()

    def fetch(n):
        at = slice(n * tile, (n + 1) * tile)
        return pltpu.make_async_copy(slots_hbm.at[:, at], slots.at[n], in_sem.at[n])

    def store(n):
        at = slice(n * tile, (n + 1) * tile)
        return pltpu.make_async_copy(out.at[n % 4], out_hbm.at[:, at], out_sem.at[n % 4])

    for n in range(parts):
        fetch(n).start()
    mix_copy.wait()
    for n in range(parts):
        fetch(n).wait()
        if n >= 4:
            store(n - 4).wait()
        out[n % 4] = jnp.dot(mix[...], slots[n], preferred_element_type=F32).astype(BF16)
        store(n).start()
    for n in range(parts - 4, parts):
        store(n).wait()


def body(tokens, block_map, slot_keys, gate_weight, up_weight, down_weight):
    _, rows, width = tokens.shape
    slots = slot_keys.shape[1]
    nseq = lax.axis_size("seq")
    ngrp = lax.axis_size("grp")
    hidden = gate_weight.shape[2]
    cw = width // CHUNKS
    bw = cw // 2
    pw = bw // SIDE
    prow = slots // 4
    per = prow // ngrp
    anywhere = pl.BlockSpec(memory_space=pltpu.HBM)
    streams = (2, 2, CHUNKS)
    dma = pltpu.SemaphoreType.DMA
    mix, seq_slots = pl.pallas_call(
        functools.partial(layer_kernel, (nseq, ngrp, 3 * slots // 4)),
        out_shape=(
            pltpu.HBM((rows, slots), BF16),
            pltpu.HBM((ngrp, 2, 2, per, width), BF16),
        ),
        in_specs=[anywhere] * 6,
        out_specs=(anywhere, anywhere),
        scratch_shapes=[
            pltpu.VMEM((rows, width), BF16),
            pltpu.SMEM(block_map.shape, jnp.int32),
            pltpu.VMEM(slot_keys.shape, BF16),
            pltpu.VMEM(gate_weight.shape, BF16),
            pltpu.VMEM(up_weight.shape, BF16),
            pltpu.VMEM(down_weight.shape, BF16),
            pltpu.VMEM((rows, slots), F32),
            pltpu.VMEM((slots, rows), BF16),
            pltpu.VMEM((rows, slots), BF16),
            pltpu.VMEM((slots, BLOCK), F32),
            pltpu.VMEM((2, SIDE, prow, BLOCK), F32),
            pltpu.VMEM((nseq, 2, slots), F32),
            pltpu.VMEM((2, 2, 2, prow, width), BF16),
            pltpu.VMEM((*streams, SIDE, prow, bw), BF16),
            pltpu.VMEM((*streams, ngrp, per, bw), BF16),
            pltpu.VMEM((*streams, SIDE * ngrp, per, pw), BF16),
            pltpu.VMEM((2, 2, prow, width), BF16),
            pltpu.VMEM((2, 2 * prow, hidden), F32),
            pltpu.VMEM((2, 2 * prow, hidden), F32),
            pltpu.VMEM((2, CHUNKS, ngrp, per, bw), BF16),
            dma((4,)),
            dma((5,)),
            dma,
            dma((2, CHUNKS)),
            dma((5, 2)),
            dma,
            dma(streams),
            dma(streams),
            dma(streams),
            dma(streams),
        ],
        compiler_params=pltpu.CompilerParams(
            collective_id=0, has_side_effects=True, vmem_limit_bytes=63 << 20
        ),
    )(
        tokens,
        pltpu.with_memory_space_constraint(block_map, pltpu.HBM),
        pltpu.with_memory_space_constraint(slot_keys, pltpu.HBM),
        gate_weight,
        up_weight,
        down_weight,
    )

    tile = width // 6
    out = pl.pallas_call(
        mix_kernel,
        out_shape=jax.ShapeDtypeStruct((rows, width), BF16),
        in_specs=[anywhere] * 2,
        out_specs=anywhere,
        scratch_shapes=[
            pltpu.VMEM((rows, slots), BF16),
            pltpu.VMEM((6, slots, tile), BF16),
            pltpu.VMEM((4, rows, tile), BF16),
            dma,
            dma((6,)),
            dma((4,)),
        ],
        compiler_params=pltpu.CompilerParams(vmem_limit_bytes=60 << 20),
    )(mix, seq_slots.reshape(slots, width))
    return out[None]


def solution(mesh):
    placed = (
        P("grp", "seq", None),
        P("grp", "seq"),
        P(),
        P("grp", None, "seq"),
        P("grp", None, "seq"),
        P("grp", "seq", None),
    )
    return jax.shard_map(
        body, mesh=mesh, in_specs=placed, out_specs=P("grp", "seq", None), check_vma=False
    )
```

```python
import functools
import jax
import jax.numpy as jnp
from jax import lax
from jax.experimental import pallas as pl
from jax.experimental.pallas import tpu as pltpu
from jax.sharding import PartitionSpec as P

BLOCK = 128
SIDE = 4
CHUNKS = 3
MESH = pl.DeviceIdType.MESH
F32 = jnp.float32
BF16 = jnp.bfloat16


def loop(start, stop, fn):
    def step(k, carry):
        fn(k)
        return carry

    lax.fori_loop(start, stop, step, 0)


def far_first(n, m):
    def hops(k):
        return min(k // m, n - k // m) + min(k % m, m - k % m)

    return sorted(range(1, n * m), key=hops, reverse=True)


def layer_kernel(
    dims,
    tok_hbm,
    bm_hbm,
    keys_hbm,
    wg_hbm,
    wu_hbm,
    wd_hbm,
    mix_hbm,
    slots_hbm,
    tok,
    bm,
    keys,
    wg,
    wu,
    wd,
    logits,
    wts,
    mixb,
    fac,
    scales,
    stat,
    terms,
    first,
    middle,
    second,
    piece_x,
    piece_y,
    counts,
    xs,
    gates,
    ups,
    ys,
    tok_sem,
    in_sem,
    mix_sem,
    own_sem,
    sent,
    stat_r,
    sum_hr,
    sum_lr,
    put_lr,
    put_hr,
    pass_hr,
):
    nseq, ngrp, image_slots = dims
    me = lax.axis_index("seq")
    grp = lax.axis_index("grp")
    level, core = grp // 2, lax.rem(grp, 2)
    levels = ngrp // 2
    rows, width = tok.shape
    slots = keys.shape[1]
    tchunk = rows // 4
    blocks = rows // BLOCK
    cw = width // CHUNKS
    bw = cw // 2
    pw = bw // SIDE
    prow = slots // 4
    per_grp = prow // ngrp
    at_x, at_y = me // SIDE, lax.rem(me, SIDE)
    place = ((at_x, at_y), (at_y, at_x))

    def seq_of(h, u, v):
        return u * SIDE + v if h == 0 else v * SIDE + u

    def block_cols(s, u):
        return pl.ds(pl.multiple_of(s * cw + lax.rem(u, 2) * bw, bw), bw)

    def piece_cols(s, u, v):
        return pl.ds(pl.multiple_of(s * cw + lax.rem(u, 2) * bw + v * pw, pw), pw)

    def piece_at(v):
        return pl.ds(pl.multiple_of(v * pw, pw), pw)

    bm_copy = pltpu.make_async_copy(bm_hbm, bm, in_sem.at[4])
    bm_copy.start()
    keys_copy = pltpu.make_async_copy(keys_hbm, keys, in_sem.at[0])
    keys_copy.start()

    def tok_copy(r):
        at = pl.ds(pl.multiple_of(r * tchunk, tchunk), tchunk)
        return pltpu.make_async_copy(tok_hbm.at[0, at], tok.at[at], tok_sem.at[r])

    loop(0, 4, lambda r: tok_copy(r).start())
    wg_copy = pltpu.make_async_copy(wg_hbm, wg, in_sem.at[1])
    wu_copy = pltpu.make_async_copy(wu_hbm, wu, in_sem.at[2])
    wd_copy = pltpu.make_async_copy(wd_hbm, wd, in_sem.at[3])

    barrier = pltpu.get_barrier_semaphore()

    def greet(peer):
        pl.semaphore_signal(barrier, inc=1, device_id=peer, device_id_type=MESH)

    for h in range(2):
        u, v = place[h]

        def greet_line(k):
            peer = seq_of(h, u, lax.rem(v + k, SIDE))
            greet({"seq": peer, "grp": level * 2 + 1 - core})

            def greet_level(n):
                greet({"seq": peer, "grp": lax.rem(level + n, levels) * 2 + core})

            loop(1, levels, greet_level)

        def greet_near(k):
            greet({"seq": seq_of(h, u, lax.rem(v + k, SIDE))})

        loop(h, SIDE, greet_line)
        loop(1, SIDE, greet_near)

    def greet_rest(k):
        x = lax.rem(at_x + 1 + k // (SIDE - 1), SIDE)
        y = lax.rem(at_y + 1 + lax.rem(k, SIDE - 1), SIDE)
        greet({"seq": x * SIDE + y})

    loop(0, (SIDE - 1) * (SIDE - 1), greet_rest)
    greeted = (2 * SIDE - 1) * levels + nseq - 1

    def to(src, dst, ssem, rsem, peer, **more):
        return pltpu.make_async_remote_copy(
            src_ref=src,
            dst_ref=dst,
            send_sem=ssem,
            recv_sem=rsem,
            device_id={"seq": peer, **more},
            device_id_type=MESH,
        )

    text_lane = (lax.broadcasted_iota(jnp.int32, (1, slots), 1) >= image_slots).astype(jnp.int32)

    def by_stream(x):
        wide = slots // 16
        return jnp.concatenate(
            [
                x[(2 * g + h) * 16 + t * 8 : (2 * g + h) * 16 + t * 8 + 8]
                for h in range(2)
                for t in range(2)
                for g in range(wide // 2)
            ],
            axis=0,
        )

    bm_copy.wait()
    keys_copy.wait()
    per = tchunk // BLOCK

    def logit_chunk(r, peak):
        tok_copy(r).wait()
        at = pl.ds(pl.multiple_of(r * tchunk, tchunk), tchunk)
        got = jnp.dot(tok[at], keys[...], preferred_element_type=F32)
        for b in range(per):
            block = jnp.where(
                text_lane == bm[0, r * per + b], got[b * BLOCK : (b + 1) * BLOCK], -1e30
            )
            logits[pl.ds(pl.multiple_of(r * tchunk + b * BLOCK, BLOCK), BLOCK)] = block
            peak = jnp.maximum(peak, jnp.max(block, axis=0, keepdims=True))
        return peak

    peak = lax.fori_loop(0, 4, logit_chunk, jnp.full((1, slots), -1e30, F32))
    wg_copy.start()
    wu_copy.start()
    wd_copy.start()

    def weigh(b, total):
        at = pl.ds(pl.multiple_of(b * BLOCK, BLOCK), BLOCK)
        w = jnp.where(text_lane == bm[0, b], jnp.exp(logits[at] - peak), 0.0)
        wts[:, at] = by_stream(w.T).astype(BF16)
        return total + jnp.sum(w, axis=0, keepdims=True)

    total = lax.fori_loop(0, blocks, weigh, jnp.zeros((1, slots), F32))
    stat[me, 0:1] = peak
    stat[me, 1:2] = total

    pl.semaphore_wait(barrier, greeted)

    def stat_copy(peer, src):
        return to(stat.at[src], stat.at[src], sent.at[0, 0], stat_r, peer)

    loop(1, nseq, lambda k: stat_copy(lax.rem(me + k, nseq), me).start())

    def around(n, at, k):
        return lax.rem(at + k, n)

    def before(n, at, k):
        return lax.rem(at + n - k, n)

    def sum_heavy(p, h, s, dst, src):
        _, v = place[h]
        return to(
            terms.at[p, h, dst // 2, :, block_cols(s, dst)],
            first.at[p, h, s, src],
            sent.at[1, p],
            sum_hr.at[p, h, s],
            seq_of(h, dst, v),
        )

    def sum_light(p, h, s, dst, dst_core, src, src_core):
        u, _ = place[h]
        return to(
            middle.at[p, h, s, :, dst_core, :, piece_at(dst)],
            second.at[p, h, s, src * 2 + src_core],
            sent.at[2, p],
            sum_lr.at[p, h, s],
            seq_of(h, u, dst),
            grp=level * 2 + dst_core,
        )

    def put_light(p, h, s, dst, dst_level, src, src_level):
        u, _ = place[h]
        if p == 0:
            here = piece_x.at[h, s, dst_level]
            at = pl.ds(pl.multiple_of(src_level * 2 * per_grp, 2 * per_grp), 2 * per_grp)
            there = xs.at[h, u // 2, at, piece_cols(s, u, src)]
        else:
            here = piece_y.at[h, s, dst_level]
            there = ys.at[h, s, src_level, :, :, piece_at(src)]
        return to(
            here,
            there,
            sent.at[3, p],
            put_lr.at[p, h, s],
            seq_of(h, u, dst),
            grp=dst_level * 2 + core,
        )

    def put_heavy(p, h, s, dst, src):
        u, v = place[h]
        if p == 0:
            here = xs.at[h, u // 2, :, block_cols(s, u)]
            there = xs.at[h, src // 2, :, block_cols(s, src)]
        else:
            here = ys.at[h, s]
            there = slots_hbm.at[:, :, h, src // 2, :, block_cols(s, src)]
        return to(
            here,
            there,
            sent.at[4, p],
            put_hr.at[p, h, s],
            seq_of(h, dst, v),
        )

    def pass_half(p, h, s, side):
        u, v = place[h]
        step = (1, SIDE - 1)[side]
        src, dst = before(SIDE, u, step), around(SIDE, u, step)
        if p == 0:
            rows_of = slice(side * prow // 2, (side + 1) * prow // 2)
            half = xs.at[h, src // 2, rows_of, block_cols(s, src)]
        else:
            levels_of = slice(side * levels // 2, (side + 1) * levels // 2)
            half = slots_hbm.at[levels_of, :, h, src // 2, :, block_cols(s, src)]
        return to(half, half, sent.at[4, p], pass_hr.at[p, h, s], seq_of(h, dst, v))

    def own_copy(h, s):
        u, _ = place[h]
        return pltpu.make_async_copy(
            ys.at[h, s],
            slots_hbm.at[:, :, h, u // 2, :, block_cols(s, u)],
            own_sem.at[h, s],
        )

    def start_sum(p, h, s):
        u, _ = place[h]
        loop(1, SIDE, lambda k: sum_heavy(p, h, s, around(SIDE, u, k), u).start())

    def arrived(ref, sem):
        pltpu.make_async_copy(ref, ref, sem).wait()

    def mid_sum(p, h, s):
        u, v = place[h]
        acc = terms[p, h, u // 2, :, block_cols(s, u)].astype(F32)
        arrived(first.at[p, h, s, : SIDE - 1], sum_hr.at[p, h, s])
        if p == 0:
            acc = acc * scale_of(h, 0)
        for k in range(1, SIDE):
            got = first[p, h, s, before(SIDE, u, k)].astype(F32)
            acc = acc + (got if p else got * scale_of(h, k))
        middle[p, h, s] = acc.reshape(middle.shape[3:]).astype(BF16)

        def send(k):
            dst, dst_core = around(SIDE, v, k // 2), lax.rem(core + k, 2)
            sum_light(p, h, s, dst, dst_core, v, core).start()

        for k in far_first(SIDE, 2):
            send(k)
        second[p, h, s, v * 2 + core] = middle[p, h, s, :, core, :, piece_at(v)]

    def scale_of(h, k):
        return jnp.concatenate([scales[h, k]] * (bw // BLOCK), axis=1)

    def end_sum(p, h, s):
        u, v = place[h]
        arrived(second.at[p, h, s, : SIDE * 2 - 1], sum_lr.at[p, h, s])
        for c in range(2):
            acc = second[p, h, s, c].astype(F32)
            for k in range(1, SIDE):
                acc = acc + second[p, h, s, 2 * k + c].astype(F32)
            if p == 0:
                piece_x[h, s, :, c * per_grp : (c + 1) * per_grp] = acc.astype(BF16)
            else:
                piece_y[h, s, :, c] = acc.astype(BF16)

        def send(k):
            dst, dst_level = around(SIDE, v, k // levels), around(levels, level, lax.rem(k, levels))
            put_light(p, h, s, dst, dst_level, v, level).start()

        for k in far_first(SIDE, levels):
            send(k)
        if p == 0:
            at = pl.ds(pl.multiple_of(level * 2 * per_grp, 2 * per_grp), 2 * per_grp)
            xs[h, u // 2, at, piece_cols(s, u, v)] = piece_x[h, s, level]
        else:
            ys[h, s, level, :, :, piece_at(v)] = piece_y[h, s, level]

    def mid_put(p, h, s):
        u, v = place[h]
        arrived(counts.at[0, : SIDE * levels - 1], put_lr.at[p, h, s])
        u, _ = place[h]
        for k in (1, 2, 3) if s == CHUNKS - 1 else (1, 3):
            put_heavy(p, h, s, around(SIDE, u, k), u).start()
        if p == 1:
            own_copy(h, s).start()

    def pass_put(p, h, s):
        arrived(first.at[p, h, s, :2], put_hr.at[p, h, s])
        for side in range(2):
            pass_half(p, h, s, side).start()

    def end_put(p, h, s):
        if s < CHUNKS - 1:
            arrived(first.at[p, h, s, 0], pass_hr.at[p, h, s])
        else:
            arrived(first.at[p, h, s, : SIDE - 1], put_hr.at[p, h, s])
        if p == 1:
            own_copy(h, s).wait()
            return
        x = xs[h, :, :, s * cw : (s + 1) * cw].reshape(2 * prow, cw)
        gate = jnp.dot(x, wg[h, s * cw : (s + 1) * cw], preferred_element_type=F32)
        up = jnp.dot(x, wu[h, s * cw : (s + 1) * cw], preferred_element_type=F32)
        if s > 0:
            gate = gate + gates[h]
            up = up + ups[h]
        if s < CHUNKS - 1:
            gates[h] = gate
            ups[h] = up
            return
        hidden = (gate / (1.0 + jnp.exp(-gate)) * up).astype(BF16)
        for n in range(CHUNKS):
            at = slice(n * cw, (n + 1) * cw)
            out = jnp.dot(hidden, wd[h, :, at], preferred_element_type=F32)
            terms[1, h, :, :, at] = out.reshape(2, prow, cw).astype(BF16)
            if n < 2:
                start_sum(1, h, n)

    def mix_rows(b):
        at = pl.ds(pl.multiple_of(b * BLOCK, BLOCK), BLOCK)
        m = logits[at]
        e = jnp.where(text_lane == bm[0, b], jnp.exp(m - jnp.max(m, axis=1, keepdims=True)), 0.0)
        mixb[at] = (e / jnp.sum(e, axis=1, keepdims=True)).astype(BF16)

    for s in range(CHUNKS):
        at = slice(s * cw, (s + 1) * cw)
        out = jnp.dot(wts[...], tok[:, at], preferred_element_type=F32)
        terms[0, :, :, :, at] = out.reshape(2, 2, prow, cw).astype(BF16)
        if s < 2:
            for h in range(2):
                start_sum(0, h, s)

    loop(0, blocks, mix_rows)
    mix_copy = pltpu.make_async_copy(mixb, mix_hbm, mix_sem)
    mix_copy.start()
    arrived(stat.at[: nseq - 1], stat_r)
    peaks = stat[:, 0, :]
    top = jnp.max(peaks, axis=0, keepdims=True)
    whole = jnp.sum(jnp.exp(peaks - top) * stat[:, 1, :], axis=0, keepdims=True)
    near = []
    for h in range(2):
        u, v = place[h]
        for k in range(SIDE):
            near.append(stat[seq_of(h, before(SIDE, u, k), v), 0:1])
    near = jnp.exp(jnp.concatenate(near, axis=0) - top) / whole
    fac[...] = by_stream(jnp.concatenate([near] * (BLOCK // (2 * SIDE)), axis=0).T)
    for h in range(2):
        u, _ = place[h]
        mine = fac[pl.ds(pl.multiple_of(h * 2 * prow + (u // 2) * prow, prow), prow)]
        for k in range(SIDE):
            scales[h, k] = jnp.broadcast_to(
                mine[:, h * SIDE + k : h * SIDE + k + 1], (prow, BLOCK)
            )

    order = (
        (mid_sum, 0),
        (start_sum, 2),
        (mid_sum, 1),
        (end_sum, 0),
        (mid_sum, 2),
        (end_sum, 1),
        (mid_put, 0),
        (end_sum, 2),
        (mid_put, 1),
        (pass_put, 0),
        (mid_put, 2),
        (pass_put, 1),
        (end_put, 0),
        (end_put, 1),
        (end_put, 2),
    )

    for p in range(2):
        for step, s in order:
            if p == 0 and (step, s) == (end_put, 0):
                wg_copy.wait()
                wu_copy.wait()
                wd_copy.wait()
            for h in range(2):
                step(p, h, s)

    mix_copy.wait()

    arrived(stat.at[: nseq - 1], sent.at[0, 0])
    for p in range(2):
        arrived(first.at[p, :, :, : SIDE - 1], sent.at[1, p])
        arrived(second.at[p, :, :, : SIDE * 2 - 1], sent.at[2, p])
        arrived(counts.at[:, : SIDE * levels - 1], sent.at[3, p])
        arrived(first.at[p, :, :, : SIDE - 1], sent.at[4, p])


def mix_kernel(mix_hbm, slots_hbm, out_hbm, mix, slots, out, mix_sem, in_sem, out_sem):
    parts, slot_count, tile = slots.shape
    mix_copy = pltpu.make_async_copy(mix_hbm, mix, mix_sem)
    mix_copy.start()

    def fetch(n):
        at = slice(n * tile, (n + 1) * tile)
        return pltpu.make_async_copy(slots_hbm.at[:, at], slots.at[n], in_sem.at[n])

    def store(n):
        at = slice(n * tile, (n + 1) * tile)
        return pltpu.make_async_copy(out.at[n % 4], out_hbm.at[:, at], out_sem.at[n % 4])

    for n in range(parts):
        fetch(n).start()
    mix_copy.wait()
    for n in range(parts):
        fetch(n).wait()
        if n >= 4:
            store(n - 4).wait()
        out[n % 4] = jnp.dot(mix[...], slots[n], preferred_element_type=F32).astype(BF16)
        store(n).start()
    for n in range(parts - 4, parts):
        store(n).wait()


def body(tokens, block_map, slot_keys, gate_weight, up_weight, down_weight):
    _, rows, width = tokens.shape
    slots = slot_keys.shape[1]
    nseq = lax.axis_size("seq")
    ngrp = lax.axis_size("grp")
    hidden = gate_weight.shape[2]
    cw = width // CHUNKS
    bw = cw // 2
    pw = bw // SIDE
    prow = slots // 4
    per = prow // ngrp
    anywhere = pl.BlockSpec(memory_space=pltpu.HBM)
    streams = (2, 2, CHUNKS)
    dma = pltpu.SemaphoreType.DMA
    mix, seq_slots = pl.pallas_call(
        functools.partial(layer_kernel, (nseq, ngrp, 3 * slots // 4)),
        out_shape=(
            pltpu.HBM((rows, slots), BF16),
            pltpu.HBM((ngrp // 2, 2, 2, 2, per, width), BF16),
        ),
        in_specs=[anywhere] * 6,
        out_specs=(anywhere, anywhere),
        scratch_shapes=[
            pltpu.VMEM((rows, width), BF16),
            pltpu.SMEM(block_map.shape, jnp.int32),
            pltpu.VMEM(slot_keys.shape, BF16),
            pltpu.VMEM(gate_weight.shape, BF16),
            pltpu.VMEM(up_weight.shape, BF16),
            pltpu.VMEM(down_weight.shape, BF16),
            pltpu.VMEM((rows, slots), F32),
            pltpu.VMEM((slots, rows), BF16),
            pltpu.VMEM((rows, slots), BF16),
            pltpu.VMEM((slots, BLOCK), F32),
            pltpu.VMEM((2, SIDE, prow, BLOCK), F32),
            pltpu.VMEM((nseq, 2, slots), F32),
            pltpu.VMEM((2, 2, 2, prow, width), BF16),
            pltpu.VMEM((*streams, SIDE, prow, bw), BF16),
            pltpu.VMEM((*streams, ngrp // 2, 2, per, bw), BF16),
            pltpu.VMEM((*streams, SIDE * 2, ngrp // 2, per, pw), BF16),
            pltpu.VMEM((2, CHUNKS, ngrp // 2, 2 * per, pw), BF16),
            pltpu.VMEM((2, CHUNKS, ngrp // 2, 2, per, pw), BF16),
            pltpu.VMEM((2 * CHUNKS, SIDE * ngrp // 2, 2 * per, pw), BF16),
            pltpu.VMEM((2, 2, prow, width), BF16),
            pltpu.VMEM((2, 2 * prow, hidden), F32),
            pltpu.VMEM((2, 2 * prow, hidden), F32),
            pltpu.VMEM((2, CHUNKS, ngrp // 2, 2, per, bw), BF16),
            dma((4,)),
            dma((5,)),
            dma,
            dma((2, CHUNKS)),
            dma((5, 2)),
            dma,
            dma(streams),
            dma(streams),
            dma(streams),
            dma(streams),
            dma(streams),
        ],
        compiler_params=pltpu.CompilerParams(
            collective_id=0, has_side_effects=True, vmem_limit_bytes=63 << 20
        ),
    )(
        tokens,
        pltpu.with_memory_space_constraint(block_map, pltpu.HBM),
        pltpu.with_memory_space_constraint(slot_keys, pltpu.HBM),
        gate_weight,
        up_weight,
        down_weight,
    )

    tile = width // 6
    out = pl.pallas_call(
        mix_kernel,
        out_shape=jax.ShapeDtypeStruct((rows, width), BF16),
        in_specs=[anywhere] * 2,
        out_specs=anywhere,
        scratch_shapes=[
            pltpu.VMEM((rows, slots), BF16),
            pltpu.VMEM((6, slots, tile), BF16),
            pltpu.VMEM((4, rows, tile), BF16),
            dma,
            dma((6,)),
            dma((4,)),
        ],
        compiler_params=pltpu.CompilerParams(vmem_limit_bytes=60 << 20),
    )(mix, seq_slots.reshape(slots, width))
    return out[None]


def solution(mesh):
    placed = (
        P("grp", "seq", None),
        P("grp", "seq"),
        P(),
        P("grp", None, "seq"),
        P("grp", None, "seq"),
        P("grp", "seq", None),
    )
    return jax.shard_map(
        body, mesh=mesh, in_specs=placed, out_specs=P("grp", "seq", None), check_vma=False
    )
```

```python
import functools
import jax
import jax.numpy as jnp
from jax import lax
from jax.experimental import pallas as pl
from jax.experimental.pallas import tpu as pltpu
from jax.sharding import PartitionSpec as P

BLOCK = 128
SIDE = 4
CHUNKS = 3
MESH = pl.DeviceIdType.MESH
F32 = jnp.float32
BF16 = jnp.bfloat16


def loop(start, stop, fn):
    def step(k, carry):
        fn(k)
        return carry

    lax.fori_loop(start, stop, step, 0)


def far_first(n, m):
    def hops(k):
        return min(k // m, n - k // m) + min(k % m, m - k % m)

    return sorted(range(1, n * m), key=hops, reverse=True)


def layer_kernel(
    dims,
    tok_hbm,
    bm_hbm,
    keys_hbm,
    wg_hbm,
    wu_hbm,
    wd_hbm,
    mix_out,
    slots_out,
    tok,
    bm,
    keys,
    wg,
    wu,
    wd,
    logits,
    wts,
    fac,
    scales,
    stat,
    terms,
    first,
    middle,
    second,
    piece_x,
    piece_y,
    counts,
    xs,
    gates,
    ups,
    ys,
    tok_sem,
    in_sem,
    own_sem,
    sent,
    stat_r,
    sum_hr,
    sum_lr,
    put_lr,
    put_hr,
    pass_hr,
):
    nseq, ngrp, image_slots = dims
    me = lax.axis_index("seq")
    grp = lax.axis_index("grp")
    level, core = grp // 2, lax.rem(grp, 2)
    levels = ngrp // 2
    rows, width = tok.shape
    slots = keys.shape[1]
    tchunk = rows // 4
    blocks = rows // BLOCK
    cw = width // CHUNKS
    bw = cw // 2
    pw = bw // SIDE
    prow = slots // 4
    per_grp = prow // ngrp
    at_x, at_y = me // SIDE, lax.rem(me, SIDE)
    place = ((at_x, at_y), (at_y, at_x))

    def seq_of(h, u, v):
        return u * SIDE + v if h == 0 else v * SIDE + u

    def block_cols(s, u):
        return pl.ds(pl.multiple_of(s * cw + lax.rem(u, 2) * bw, bw), bw)

    def piece_cols(s, u, v):
        return pl.ds(pl.multiple_of(s * cw + lax.rem(u, 2) * bw + v * pw, pw), pw)

    def piece_at(v):
        return pl.ds(pl.multiple_of(v * pw, pw), pw)

    bm_copy = pltpu.make_async_copy(bm_hbm, bm, in_sem.at[4])
    bm_copy.start()
    keys_copy = pltpu.make_async_copy(keys_hbm, keys, in_sem.at[0])
    keys_copy.start()

    def tok_copy(r):
        at = pl.ds(pl.multiple_of(r * tchunk, tchunk), tchunk)
        return pltpu.make_async_copy(tok_hbm.at[0, at], tok.at[at], tok_sem.at[r])

    loop(0, 4, lambda r: tok_copy(r).start())
    wg_copy = pltpu.make_async_copy(wg_hbm, wg, in_sem.at[1])
    wu_copy = pltpu.make_async_copy(wu_hbm, wu, in_sem.at[2])
    wd_copy = pltpu.make_async_copy(wd_hbm, wd, in_sem.at[3])

    barrier = pltpu.get_barrier_semaphore()

    def greet(peer):
        pl.semaphore_signal(barrier, inc=1, device_id=peer, device_id_type=MESH)

    for h in range(2):
        u, v = place[h]

        def greet_line(k):
            peer = seq_of(h, u, lax.rem(v + k, SIDE))
            greet({"seq": peer, "grp": level * 2 + 1 - core})

            def greet_level(n):
                greet({"seq": peer, "grp": lax.rem(level + n, levels) * 2 + core})

            loop(1, levels, greet_level)

        def greet_near(k):
            greet({"seq": seq_of(h, u, lax.rem(v + k, SIDE))})

        loop(h, SIDE, greet_line)
        loop(1, SIDE, greet_near)

    def greet_rest(k):
        x = lax.rem(at_x + 1 + k // (SIDE - 1), SIDE)
        y = lax.rem(at_y + 1 + lax.rem(k, SIDE - 1), SIDE)
        greet({"seq": x * SIDE + y})

    loop(0, (SIDE - 1) * (SIDE - 1), greet_rest)
    greeted = (2 * SIDE - 1) * levels + nseq - 1

    def to(src, dst, ssem, rsem, peer, **more):
        return pltpu.make_async_remote_copy(
            src_ref=src,
            dst_ref=dst,
            send_sem=ssem,
            recv_sem=rsem,
            device_id={"seq": peer, **more},
            device_id_type=MESH,
        )

    text_lane = (lax.broadcasted_iota(jnp.int32, (1, slots), 1) >= image_slots).astype(jnp.int32)

    def by_stream(x):
        wide = slots // 16
        return jnp.concatenate(
            [
                x[(2 * g + h) * 16 + t * 8 : (2 * g + h) * 16 + t * 8 + 8]
                for h in range(2)
                for t in range(2)
                for g in range(wide // 2)
            ],
            axis=0,
        )

    bm_copy.wait()
    keys_copy.wait()
    per = tchunk // BLOCK

    def logit_chunk(r, peak):
        tok_copy(r).wait()
        at = pl.ds(pl.multiple_of(r * tchunk, tchunk), tchunk)
        got = jnp.dot(tok[at], keys[...], preferred_element_type=F32)
        for b in range(per):
            block = jnp.where(
                text_lane == bm[0, r * per + b], got[b * BLOCK : (b + 1) * BLOCK], -1e30
            )
            logits[pl.ds(pl.multiple_of(r * tchunk + b * BLOCK, BLOCK), BLOCK)] = block
            peak = jnp.maximum(peak, jnp.max(block, axis=0, keepdims=True))
        return peak

    peak = lax.fori_loop(0, 4, logit_chunk, jnp.full((1, slots), -1e30, F32))
    wg_copy.start()
    wu_copy.start()
    wd_copy.start()

    def weigh(b, total):
        at = pl.ds(pl.multiple_of(b * BLOCK, BLOCK), BLOCK)
        w = jnp.where(text_lane == bm[0, b], jnp.exp(logits[at] - peak), 0.0)
        wts[:, at] = by_stream(w.T).astype(BF16)
        return total + jnp.sum(w, axis=0, keepdims=True)

    total = lax.fori_loop(0, blocks, weigh, jnp.zeros((1, slots), F32))
    stat[me, 0:1] = peak
    stat[me, 1:2] = total

    pl.semaphore_wait(barrier, greeted)

    def stat_copy(peer, src):
        return to(stat.at[src], stat.at[src], sent.at[0, 0], stat_r, peer)

    loop(1, nseq, lambda k: stat_copy(lax.rem(me + k, nseq), me).start())

    def around(n, at, k):
        return lax.rem(at + k, n)

    def before(n, at, k):
        return lax.rem(at + n - k, n)

    def sum_heavy(p, h, s, dst, src):
        _, v = place[h]
        return to(
            terms.at[p, h, dst // 2, :, block_cols(s, dst)],
            first.at[p, h, s, src],
            sent.at[1, p],
            sum_hr.at[p, h, s],
            seq_of(h, dst, v),
        )

    def sum_light(p, h, s, dst, dst_core, src, src_core):
        u, _ = place[h]
        return to(
            middle.at[p, h, s, :, dst_core, :, piece_at(dst)],
            second.at[p, h, s, src * 2 + src_core],
            sent.at[2, p],
            sum_lr.at[p, h, s],
            seq_of(h, u, dst),
            grp=level * 2 + dst_core,
        )

    def put_light(p, h, s, dst, dst_level, src, src_level):
        u, _ = place[h]
        if p == 0:
            here = piece_x.at[h, s, dst_level]
            at = pl.ds(pl.multiple_of(src_level * 2 * per_grp, 2 * per_grp), 2 * per_grp)
            there = xs.at[h, u // 2, at, piece_cols(s, u, src)]
        else:
            here = piece_y.at[h, s, dst_level]
            there = ys.at[h, s, src_level, :, :, piece_at(src)]
        return to(
            here,
            there,
            sent.at[3, p],
            put_lr.at[p, h, s],
            seq_of(h, u, dst),
            grp=dst_level * 2 + core,
        )

    def put_heavy(p, h, s, dst, src):
        u, v = place[h]
        if p == 0:
            here = xs.at[h, u // 2, :, block_cols(s, u)]
            there = xs.at[h, src // 2, :, block_cols(s, src)]
        else:
            here = ys.at[h, s]
            there = slots_out.at[:, :, h, src // 2, :, block_cols(s, src)]
        return to(
            here,
            there,
            sent.at[4, p],
            put_hr.at[p, h, s],
            seq_of(h, dst, v),
        )

    def pass_half(p, h, s, side):
        u, v = place[h]
        step = (1, SIDE - 1)[side]
        src, dst = before(SIDE, u, step), around(SIDE, u, step)
        if p == 0:
            rows_of = slice(side * prow // 2, (side + 1) * prow // 2)
            half = xs.at[h, src // 2, rows_of, block_cols(s, src)]
        else:
            levels_of = slice(side * levels // 2, (side + 1) * levels // 2)
            half = slots_out.at[levels_of, :, h, src // 2, :, block_cols(s, src)]
        return to(half, half, sent.at[4, p], pass_hr.at[p, h, s], seq_of(h, dst, v))

    def own_copy(h, s):
        u, _ = place[h]
        return pltpu.make_async_copy(
            ys.at[h, s],
            slots_out.at[:, :, h, u // 2, :, block_cols(s, u)],
            own_sem.at[h, s],
        )

    def start_sum(p, h, s):
        u, _ = place[h]
        loop(1, SIDE, lambda k: sum_heavy(p, h, s, around(SIDE, u, k), u).start())

    def arrived(ref, sem):
        pltpu.make_async_copy(ref, ref, sem).wait()

    def mid_sum(p, h, s):
        u, v = place[h]
        acc = terms[p, h, u // 2, :, block_cols(s, u)].astype(F32)
        arrived(first.at[p, h, s, : SIDE - 1], sum_hr.at[p, h, s])
        if p == 0:
            acc = acc * scale_of(h, 0)
        for k in range(1, SIDE):
            got = first[p, h, s, before(SIDE, u, k)].astype(F32)
            acc = acc + (got if p else got * scale_of(h, k))
        middle[p, h, s] = acc.reshape(middle.shape[3:]).astype(BF16)

        def send(k):
            dst, dst_core = around(SIDE, v, k // 2), lax.rem(core + k, 2)
            sum_light(p, h, s, dst, dst_core, v, core).start()

        for k in far_first(SIDE, 2):
            send(k)
        second[p, h, s, v * 2 + core] = middle[p, h, s, :, core, :, piece_at(v)]

    def scale_of(h, k):
        return jnp.concatenate([scales[h, k]] * (bw // BLOCK), axis=1)

    def end_sum(p, h, s):
        u, v = place[h]
        arrived(second.at[p, h, s, : SIDE * 2 - 1], sum_lr.at[p, h, s])
        for c in range(2):
            acc = second[p, h, s, c].astype(F32)
            for k in range(1, SIDE):
                acc = acc + second[p, h, s, 2 * k + c].astype(F32)
            if p == 0:
                piece_x[h, s, :, c * per_grp : (c + 1) * per_grp] = acc.astype(BF16)
            else:
                piece_y[h, s, :, c] = acc.astype(BF16)

        def send(k):
            dst, dst_level = around(SIDE, v, k // levels), around(levels, level, lax.rem(k, levels))
            put_light(p, h, s, dst, dst_level, v, level).start()

        for k in far_first(SIDE, levels):
            send(k)
        if p == 0:
            at = pl.ds(pl.multiple_of(level * 2 * per_grp, 2 * per_grp), 2 * per_grp)
            xs[h, u // 2, at, piece_cols(s, u, v)] = piece_x[h, s, level]
        else:
            ys[h, s, level, :, :, piece_at(v)] = piece_y[h, s, level]

    def mid_put(p, h, s):
        u, v = place[h]
        arrived(counts.at[0, : SIDE * levels - 1], put_lr.at[p, h, s])
        u, _ = place[h]
        for k in (1, 2, 3) if s == CHUNKS - 1 else (1, 3):
            put_heavy(p, h, s, around(SIDE, u, k), u).start()
        if p == 1:
            own_copy(h, s).start()

    def pass_put(p, h, s):
        arrived(first.at[p, h, s, :2], put_hr.at[p, h, s])
        for side in range(2):
            pass_half(p, h, s, side).start()

    def end_put(p, h, s):
        if s < CHUNKS - 1:
            arrived(first.at[p, h, s, 0], pass_hr.at[p, h, s])
        else:
            arrived(first.at[p, h, s, : SIDE - 1], put_hr.at[p, h, s])
        if p == 1:
            own_copy(h, s).wait()
            return
        x = xs[h, :, :, s * cw : (s + 1) * cw].reshape(2 * prow, cw)
        gate = jnp.dot(x, wg[h, s * cw : (s + 1) * cw], preferred_element_type=F32)
        up = jnp.dot(x, wu[h, s * cw : (s + 1) * cw], preferred_element_type=F32)
        if s > 0:
            gate = gate + gates[h]
            up = up + ups[h]
        if s < CHUNKS - 1:
            gates[h] = gate
            ups[h] = up
            return
        hidden = (gate / (1.0 + jnp.exp(-gate)) * up).astype(BF16)
        for n in range(CHUNKS):
            at = slice(n * cw, (n + 1) * cw)
            out = jnp.dot(hidden, wd[h, :, at], preferred_element_type=F32)
            terms[1, h, :, :, at] = out.reshape(2, prow, cw).astype(BF16)
            if n < 2:
                start_sum(1, h, n)

    def mix_rows(b):
        at = pl.ds(pl.multiple_of(b * BLOCK, BLOCK), BLOCK)
        m = logits[at]
        e = jnp.where(text_lane == bm[0, b], jnp.exp(m - jnp.max(m, axis=1, keepdims=True)), 0.0)
        mix_out[at] = (e / jnp.sum(e, axis=1, keepdims=True)).astype(BF16)

    for s in range(CHUNKS):
        at = slice(s * cw, (s + 1) * cw)
        out = jnp.dot(wts[...], tok[:, at], preferred_element_type=F32)
        terms[0, :, :, :, at] = out.reshape(2, 2, prow, cw).astype(BF16)
        if s < 2:
            for h in range(2):
                start_sum(0, h, s)

    loop(0, blocks, mix_rows)
    arrived(stat.at[: nseq - 1], stat_r)
    peaks = stat[:, 0, :]
    top = jnp.max(peaks, axis=0, keepdims=True)
    whole = jnp.sum(jnp.exp(peaks - top) * stat[:, 1, :], axis=0, keepdims=True)
    near = []
    for h in range(2):
        u, v = place[h]
        for k in range(SIDE):
            near.append(stat[seq_of(h, before(SIDE, u, k), v), 0:1])
    near = jnp.exp(jnp.concatenate(near, axis=0) - top) / whole
    fac[...] = by_stream(jnp.concatenate([near] * (BLOCK // (2 * SIDE)), axis=0).T)
    for h in range(2):
        u, _ = place[h]
        mine = fac[pl.ds(pl.multiple_of(h * 2 * prow + (u // 2) * prow, prow), prow)]
        for k in range(SIDE):
            scales[h, k] = jnp.broadcast_to(
                mine[:, h * SIDE + k : h * SIDE + k + 1], (prow, BLOCK)
            )

    order = (
        (mid_sum, 0),
        (start_sum, 2),
        (mid_sum, 1),
        (end_sum, 0),
        (mid_sum, 2),
        (end_sum, 1),
        (mid_put, 0),
        (end_sum, 2),
        (mid_put, 1),
        (pass_put, 0),
        (mid_put, 2),
        (pass_put, 1),
        (end_put, 0),
        (end_put, 1),
        (end_put, 2),
    )

    for p in range(2):
        for step, s in order:
            if p == 0 and (step, s) == (end_put, 0):
                wg_copy.wait()
                wu_copy.wait()
                wd_copy.wait()
            for h in range(2):
                step(p, h, s)


    arrived(stat.at[: nseq - 1], sent.at[0, 0])
    for p in range(2):
        arrived(first.at[p, :, :, : SIDE - 1], sent.at[1, p])
        arrived(second.at[p, :, :, : SIDE * 2 - 1], sent.at[2, p])
        arrived(counts.at[:, : SIDE * levels - 1], sent.at[3, p])
        arrived(first.at[p, :, :, : SIDE - 1], sent.at[4, p])


def mix_kernel(mix, slots, out_hbm, out, out_sem):
    tile = out.shape[2]
    parts = slots.shape[1] // tile

    def store(n):
        at = slice(n * tile, (n + 1) * tile)
        return pltpu.make_async_copy(out.at[n % 4], out_hbm.at[:, at], out_sem.at[n % 4])

    for n in range(parts):
        if n >= 4:
            store(n - 4).wait()
        out[n % 4] = jnp.dot(
            mix[...], slots[:, n * tile : (n + 1) * tile], preferred_element_type=F32
        ).astype(BF16)
        store(n).start()
    for n in range(parts - 4, parts):
        store(n).wait()


def body(tokens, block_map, slot_keys, gate_weight, up_weight, down_weight):
    _, rows, width = tokens.shape
    slots = slot_keys.shape[1]
    nseq = lax.axis_size("seq")
    ngrp = lax.axis_size("grp")
    hidden = gate_weight.shape[2]
    cw = width // CHUNKS
    bw = cw // 2
    pw = bw // SIDE
    prow = slots // 4
    per = prow // ngrp
    anywhere = pl.BlockSpec(memory_space=pltpu.HBM)
    on_chip = pl.BlockSpec(memory_space=pltpu.VMEM)
    streams = (2, 2, CHUNKS)
    dma = pltpu.SemaphoreType.DMA
    mix, seq_slots = pl.pallas_call(
        functools.partial(layer_kernel, (nseq, ngrp, 3 * slots // 4)),
        out_shape=(
            pltpu.VMEM((rows, slots), BF16),
            pltpu.VMEM((ngrp // 2, 2, 2, 2, per, width), BF16),
        ),
        in_specs=[anywhere] * 6,
        out_specs=(on_chip, on_chip),
        scratch_shapes=[
            pltpu.VMEM((rows, width), BF16),
            pltpu.SMEM(block_map.shape, jnp.int32),
            pltpu.VMEM(slot_keys.shape, BF16),
            pltpu.VMEM(gate_weight.shape, BF16),
            pltpu.VMEM(up_weight.shape, BF16),
            pltpu.VMEM(down_weight.shape, BF16),
            pltpu.VMEM((rows, slots), F32),
            pltpu.VMEM((slots, rows), BF16),
            pltpu.VMEM((slots, BLOCK), F32),
            pltpu.VMEM((2, SIDE, prow, BLOCK), F32),
            pltpu.VMEM((nseq, 2, slots), F32),
            pltpu.VMEM((2, 2, 2, prow, width), BF16),
            pltpu.VMEM((*streams, SIDE, prow, bw), BF16),
            pltpu.VMEM((*streams, ngrp // 2, 2, per, bw), BF16),
            pltpu.VMEM((*streams, SIDE * 2, ngrp // 2, per, pw), BF16),
            pltpu.VMEM((2, CHUNKS, ngrp // 2, 2 * per, pw), BF16),
            pltpu.VMEM((2, CHUNKS, ngrp // 2, 2, per, pw), BF16),
            pltpu.VMEM((2 * CHUNKS, SIDE * ngrp // 2, 2 * per, pw), BF16),
            pltpu.VMEM((2, 2, prow, width), BF16),
            pltpu.VMEM((2, 2 * prow, hidden), F32),
            pltpu.VMEM((2, 2 * prow, hidden), F32),
            pltpu.VMEM((2, CHUNKS, ngrp // 2, 2, per, bw), BF16),
            dma((4,)),
            dma((5,)),
            dma((2, CHUNKS)),
            dma((5, 2)),
            dma,
            dma(streams),
            dma(streams),
            dma(streams),
            dma(streams),
            dma(streams),
        ],
        compiler_params=pltpu.CompilerParams(
            collective_id=0, has_side_effects=True, vmem_limit_bytes=56 << 20
        ),
    )(
        *(
            pltpu.with_memory_space_constraint(x, pltpu.HBM)
            for x in (tokens, block_map, slot_keys, gate_weight, up_weight, down_weight)
        )
    )

    tile = width // 6
    out = pl.pallas_call(
        mix_kernel,
        out_shape=jax.ShapeDtypeStruct((rows, width), BF16),
        in_specs=[on_chip] * 2,
        out_specs=anywhere,
        scratch_shapes=[pltpu.VMEM((4, rows, tile), BF16), dma((4,))],
        compiler_params=pltpu.CompilerParams(vmem_limit_bytes=32 << 20),
    )(mix, seq_slots.reshape(slots, width))
    return out[None]


def solution(mesh):
    placed = (
        P("grp", "seq", None),
        P("grp", "seq"),
        P(),
        P("grp", None, "seq"),
        P("grp", None, "seq"),
        P("grp", "seq", None),
    )
    return jax.shard_map(
        body, mesh=mesh, in_specs=placed, out_specs=P("grp", "seq", None), check_vma=False
    )
```

```python
import functools
import jax
import jax.numpy as jnp
from jax import lax
from jax.experimental import pallas as pl
from jax.experimental.pallas import tpu as pltpu
from jax.sharding import PartitionSpec as P

BLOCK = 128
SIDE = 4
CHUNKS = 3
MESH = pl.DeviceIdType.MESH
F32 = jnp.float32
BF16 = jnp.bfloat16


def loop(start, stop, fn):
    def step(k, carry):
        fn(k)
        return carry

    lax.fori_loop(start, stop, step, 0)


def far_first(n, m):
    def hops(k):
        return min(k // m, n - k // m) + min(k % m, m - k % m)

    return sorted(range(1, n * m), key=hops, reverse=True)


def layer_kernel(
    dims,
    tok_hbm,
    bm_hbm,
    keys_hbm,
    wg_hbm,
    wu_hbm,
    wd_hbm,
    mix_out,
    slots_out,
    tok,
    bm,
    keys,
    wg,
    wu,
    wd,
    logits,
    wts,
    fac,
    scales,
    stat,
    terms,
    first,
    middle,
    second,
    piece_x,
    piece_y,
    counts,
    xs,
    gates,
    ups,
    ys,
    tok_sem,
    in_sem,
    own_sem,
    sent,
    stat_r,
    sum_hr,
    sum_lr,
    put_lr,
    put_hr,
    pass_hr,
):
    nseq, ngrp, image_slots = dims
    me = lax.axis_index("seq")
    grp = lax.axis_index("grp")
    level, core = grp // 2, lax.rem(grp, 2)
    levels = ngrp // 2
    rows, width = tok.shape
    slots = keys.shape[1]
    tchunk = rows // 4
    blocks = rows // BLOCK
    cw = width // CHUNKS
    bw = cw // 2
    pw = bw // SIDE
    prow = slots // 4
    per_grp = prow // ngrp
    at_x, at_y = me // SIDE, lax.rem(me, SIDE)
    place = ((at_x, at_y), (at_y, at_x))

    def seq_of(h, u, v):
        return u * SIDE + v if h == 0 else v * SIDE + u

    def block_cols(s, u):
        return pl.ds(pl.multiple_of(s * cw + lax.rem(u, 2) * bw, bw), bw)

    def piece_cols(s, u, v):
        return pl.ds(pl.multiple_of(s * cw + lax.rem(u, 2) * bw + v * pw, pw), pw)

    def piece_at(v):
        return pl.ds(pl.multiple_of(v * pw, pw), pw)

    bm_copy = pltpu.make_async_copy(bm_hbm, bm, in_sem.at[4])
    bm_copy.start()
    keys_copy = pltpu.make_async_copy(keys_hbm, keys, in_sem.at[0])
    keys_copy.start()

    def tok_copy(r):
        at = pl.ds(pl.multiple_of(r * tchunk, tchunk), tchunk)
        return pltpu.make_async_copy(tok_hbm.at[0, at], tok.at[at], tok_sem.at[r])

    loop(0, 4, lambda r: tok_copy(r).start())
    wg_copy = pltpu.make_async_copy(wg_hbm, wg, in_sem.at[1])
    wu_copy = pltpu.make_async_copy(wu_hbm, wu, in_sem.at[2])
    wd_copy = pltpu.make_async_copy(wd_hbm, wd, in_sem.at[3])

    barrier = pltpu.get_barrier_semaphore()

    def greet(peer):
        pl.semaphore_signal(barrier, inc=1, device_id=peer, device_id_type=MESH)

    for h in range(2):
        u, v = place[h]

        def greet_line(k):
            peer = seq_of(h, u, lax.rem(v + k, SIDE))
            greet({"seq": peer, "grp": level * 2 + 1 - core})

            def greet_level(n):
                greet({"seq": peer, "grp": lax.rem(level + n, levels) * 2 + core})

            loop(1, levels, greet_level)

        def greet_near(k):
            greet({"seq": seq_of(h, u, lax.rem(v + k, SIDE))})

        loop(h, SIDE, greet_line)
        loop(1, SIDE, greet_near)

    def greet_rest(k):
        x = lax.rem(at_x + 1 + k // (SIDE - 1), SIDE)
        y = lax.rem(at_y + 1 + lax.rem(k, SIDE - 1), SIDE)
        greet({"seq": x * SIDE + y})

    loop(0, (SIDE - 1) * (SIDE - 1), greet_rest)
    greeted = (2 * SIDE - 1) * levels + nseq - 1

    def to(src, dst, ssem, rsem, peer, **more):
        return pltpu.make_async_remote_copy(
            src_ref=src,
            dst_ref=dst,
            send_sem=ssem,
            recv_sem=rsem,
            device_id={"seq": peer, **more},
            device_id_type=MESH,
        )

    text_lane = (lax.broadcasted_iota(jnp.int32, (1, slots), 1) >= image_slots).astype(jnp.int32)

    def by_stream(x):
        wide = slots // 16
        return jnp.concatenate(
            [
                x[(2 * g + h) * 16 + t * 8 : (2 * g + h) * 16 + t * 8 + 8]
                for h in range(2)
                for t in range(2)
                for g in range(wide // 2)
            ],
            axis=0,
        )

    bm_copy.wait()
    keys_copy.wait()
    per = tchunk // BLOCK

    def logit_chunk(r, peak):
        tok_copy(r).wait()
        at = pl.ds(pl.multiple_of(r * tchunk, tchunk), tchunk)
        got = jnp.dot(tok[at], keys[...], preferred_element_type=F32)
        for b in range(per):
            block = jnp.where(
                text_lane == bm[0, r * per + b], got[b * BLOCK : (b + 1) * BLOCK], -1e30
            )
            logits[pl.ds(pl.multiple_of(r * tchunk + b * BLOCK, BLOCK), BLOCK)] = block
            peak = jnp.maximum(peak, jnp.max(block, axis=0, keepdims=True))
        return peak

    peak = lax.fori_loop(0, 4, logit_chunk, jnp.full((1, slots), -1e30, F32))
    wg_copy.start()
    wu_copy.start()
    wd_copy.start()

    def weigh(b, total):
        at = pl.ds(pl.multiple_of(b * BLOCK, BLOCK), BLOCK)
        w = jnp.where(text_lane == bm[0, b], jnp.exp(logits[at] - peak), 0.0)
        wts[:, at] = by_stream(w.T).astype(BF16)
        return total + jnp.sum(w, axis=0, keepdims=True)

    total = lax.fori_loop(0, blocks, weigh, jnp.zeros((1, slots), F32))
    stat[me, 0:1] = peak
    stat[me, 1:2] = total

    pl.semaphore_wait(barrier, greeted)

    def stat_copy(peer, src):
        return to(stat.at[src], stat.at[src], sent.at[0, 0], stat_r, peer)

    loop(1, nseq, lambda k: stat_copy(lax.rem(me + k, nseq), me).start())

    def around(n, at, k):
        return lax.rem(at + k, n)

    def before(n, at, k):
        return lax.rem(at + n - k, n)

    def sum_heavy(p, h, s, dst, src):
        _, v = place[h]
        return to(
            terms.at[p, h, dst // 2, :, block_cols(s, dst)],
            first.at[p, h, s, src],
            sent.at[1, p],
            sum_hr.at[p, h, s],
            seq_of(h, dst, v),
        )

    def sum_light(p, h, s, dst, dst_core, src, src_core):
        u, _ = place[h]
        return to(
            middle.at[p, h, s, :, dst_core, :, piece_at(dst)],
            second.at[p, h, s, src * 2 + src_core],
            sent.at[2, p],
            sum_lr.at[p, h, s],
            seq_of(h, u, dst),
            grp=level * 2 + dst_core,
        )

    def put_light(p, h, s, dst, dst_level, src, src_level):
        u, _ = place[h]
        if p == 0:
            here = piece_x.at[h, s, dst_level]
            at = pl.ds(pl.multiple_of(src_level * 2 * per_grp, 2 * per_grp), 2 * per_grp)
            there = xs.at[h, u // 2, at, piece_cols(s, u, src)]
        else:
            here = piece_y.at[h, s, dst_level]
            there = ys.at[h, s, src_level, :, :, piece_at(src)]
        return to(
            here,
            there,
            sent.at[3, p],
            put_lr.at[p, h, s],
            seq_of(h, u, dst),
            grp=dst_level * 2 + core,
        )

    def put_heavy(p, h, s, dst, src):
        u, v = place[h]
        if p == 0:
            here = xs.at[h, u // 2, :, block_cols(s, u)]
            there = xs.at[h, src // 2, :, block_cols(s, src)]
        else:
            here = ys.at[h, s]
            there = slots_out.at[:, :, h, src // 2, :, block_cols(s, src)]
        return to(
            here,
            there,
            sent.at[4, p],
            put_hr.at[p, h, s],
            seq_of(h, dst, v),
        )

    def pass_half(p, h, s, side):
        u, v = place[h]
        step = (1, SIDE - 1)[side]
        src, dst = before(SIDE, u, step), around(SIDE, u, step)
        if p == 0:
            rows_of = slice(side * prow // 2, (side + 1) * prow // 2)
            half = xs.at[h, src // 2, rows_of, block_cols(s, src)]
        else:
            levels_of = slice(side * levels // 2, (side + 1) * levels // 2)
            half = slots_out.at[levels_of, :, h, src // 2, :, block_cols(s, src)]
        return to(half, half, sent.at[4, p], pass_hr.at[p, h, s], seq_of(h, dst, v))

    def own_copy(h, s):
        u, _ = place[h]
        return pltpu.make_async_copy(
            ys.at[h, s],
            slots_out.at[:, :, h, u // 2, :, block_cols(s, u)],
            own_sem.at[h, s],
        )

    def start_sum(p, h, s):
        u, _ = place[h]
        loop(1, SIDE, lambda k: sum_heavy(p, h, s, around(SIDE, u, k), u).start())

    def arrived(ref, sem):
        pltpu.make_async_copy(ref, ref, sem).wait()

    def mid_sum(p, h, s):
        u, v = place[h]
        acc = terms[p, h, u // 2, :, block_cols(s, u)].astype(F32)
        arrived(first.at[p, h, s, : SIDE - 1], sum_hr.at[p, h, s])
        if p == 0:
            acc = acc * scale_of(h, 0)
        for k in range(1, SIDE):
            got = first[p, h, s, before(SIDE, u, k)].astype(F32)
            acc = acc + (got if p else got * scale_of(h, k))
        middle[p, h, s] = acc.reshape(middle.shape[3:]).astype(BF16)

        def send(k):
            dst, dst_core = around(SIDE, v, k // 2), lax.rem(core + k, 2)
            sum_light(p, h, s, dst, dst_core, v, core).start()

        for k in far_first(SIDE, 2):
            send(k)
        second[p, h, s, v * 2 + core] = middle[p, h, s, :, core, :, piece_at(v)]

    def scale_of(h, k):
        return jnp.concatenate([scales[h, k]] * (bw // BLOCK), axis=1)

    def end_sum(p, h, s):
        u, v = place[h]
        arrived(second.at[p, h, s, : SIDE * 2 - 1], sum_lr.at[p, h, s])
        for c in range(2):
            acc = second[p, h, s, c].astype(F32)
            for k in range(1, SIDE):
                acc = acc + second[p, h, s, 2 * k + c].astype(F32)
            if p == 0:
                piece_x[h, s, :, c * per_grp : (c + 1) * per_grp] = acc.astype(BF16)
            else:
                piece_y[h, s, :, c] = acc.astype(BF16)

        def send(k):
            dst, dst_level = around(SIDE, v, k // levels), around(levels, level, lax.rem(k, levels))
            put_light(p, h, s, dst, dst_level, v, level).start()

        for k in far_first(SIDE, levels):
            send(k)
        if p == 0:
            at = pl.ds(pl.multiple_of(level * 2 * per_grp, 2 * per_grp), 2 * per_grp)
            xs[h, u // 2, at, piece_cols(s, u, v)] = piece_x[h, s, level]
        else:
            ys[h, s, level, :, :, piece_at(v)] = piece_y[h, s, level]

    def mid_put(p, h, s):
        u, v = place[h]
        arrived(counts.at[0, : SIDE * levels - 1], put_lr.at[p, h, s])
        u, _ = place[h]
        for k in (1, 2, 3) if s == CHUNKS - 1 else (1, 3):
            put_heavy(p, h, s, around(SIDE, u, k), u).start()
        if p == 1:
            own_copy(h, s).start()

    def pass_put(p, h, s):
        arrived(first.at[p, h, s, :2], put_hr.at[p, h, s])
        for side in range(2):
            pass_half(p, h, s, side).start()

    def end_put(p, h, s):
        if s < CHUNKS - 1:
            arrived(first.at[p, h, s, 0], pass_hr.at[p, h, s])
        else:
            arrived(first.at[p, h, s, : SIDE - 1], put_hr.at[p, h, s])
        if p == 1:
            own_copy(h, s).wait()
            return
        x = xs[h, :, :, s * cw : (s + 1) * cw].reshape(2 * prow, cw)
        gate = jnp.dot(x, wg[h, s * cw : (s + 1) * cw], preferred_element_type=F32)
        up = jnp.dot(x, wu[h, s * cw : (s + 1) * cw], preferred_element_type=F32)
        if s > 0:
            gate = gate + gates[h]
            up = up + ups[h]
        if s < CHUNKS - 1:
            gates[h] = gate
            ups[h] = up
            return
        gates[h] = gate / (1.0 + jnp.exp(-gate)) * up
        if h == 0:
            return
        for n in range(CHUNKS):
            for e in range(2):
                at = slice(n * cw, (n + 1) * cw)
                out = jnp.dot(gates[e].astype(BF16), wd[e, :, at], preferred_element_type=F32)
                terms[1, e, :, :, at] = out.reshape(2, prow, cw).astype(BF16)
                if n < 2:
                    start_sum(1, e, n)

    def mix_rows(b):
        at = pl.ds(pl.multiple_of(b * BLOCK, BLOCK), BLOCK)
        m = logits[at]
        e = jnp.where(text_lane == bm[0, b], jnp.exp(m - jnp.max(m, axis=1, keepdims=True)), 0.0)
        mix_out[at] = (e / jnp.sum(e, axis=1, keepdims=True)).astype(BF16)

    for s in range(CHUNKS):
        at = slice(s * cw, (s + 1) * cw)
        out = jnp.dot(wts[...], tok[:, at], preferred_element_type=F32)
        terms[0, :, :, :, at] = out.reshape(2, 2, prow, cw).astype(BF16)
        if s < 2:
            for h in range(2):
                start_sum(0, h, s)

    loop(0, blocks, mix_rows)
    arrived(stat.at[: nseq - 1], stat_r)
    peaks = stat[:, 0, :]
    top = jnp.max(peaks, axis=0, keepdims=True)
    whole = jnp.sum(jnp.exp(peaks - top) * stat[:, 1, :], axis=0, keepdims=True)
    near = []
    for h in range(2):
        u, v = place[h]
        for k in range(SIDE):
            near.append(stat[seq_of(h, before(SIDE, u, k), v), 0:1])
    near = jnp.exp(jnp.concatenate(near, axis=0) - top) / whole
    fac[...] = by_stream(jnp.concatenate([near] * (BLOCK // (2 * SIDE)), axis=0).T)
    for h in range(2):
        u, _ = place[h]
        mine = fac[pl.ds(pl.multiple_of(h * 2 * prow + (u // 2) * prow, prow), prow)]
        for k in range(SIDE):
            scales[h, k] = jnp.broadcast_to(
                mine[:, h * SIDE + k : h * SIDE + k + 1], (prow, BLOCK)
            )

    order = (
        (mid_sum, 0),
        (start_sum, 2),
        (mid_sum, 1),
        (end_sum, 0),
        (mid_sum, 2),
        (end_sum, 1),
        (mid_put, 0),
        (end_sum, 2),
        (mid_put, 1),
        (pass_put, 0),
        (mid_put, 2),
        (pass_put, 1),
        (end_put, 0),
        (end_put, 1),
        (end_put, 2),
    )

    for p in range(2):
        for step, s in order:
            if p == 0 and (step, s) == (end_put, 0):
                wg_copy.wait()
                wu_copy.wait()
                wd_copy.wait()
            for h in range(2):
                step(p, h, s)


    arrived(stat.at[: nseq - 1], sent.at[0, 0])
    for p in range(2):
        arrived(first.at[p, :, :, : SIDE - 1], sent.at[1, p])
        arrived(second.at[p, :, :, : SIDE * 2 - 1], sent.at[2, p])
        arrived(counts.at[:, : SIDE * levels - 1], sent.at[3, p])
        arrived(first.at[p, :, :, : SIDE - 1], sent.at[4, p])


def mix_kernel(mix, slots, out_hbm, out, out_sem):
    tile = out.shape[2]
    parts = slots.shape[1] // tile

    def store(n):
        at = slice(n * tile, (n + 1) * tile)
        return pltpu.make_async_copy(out.at[n % 4], out_hbm.at[:, at], out_sem.at[n % 4])

    for n in range(parts):
        if n >= 4:
            store(n - 4).wait()
        out[n % 4] = jnp.dot(
            mix[...], slots[:, n * tile : (n + 1) * tile], preferred_element_type=F32
        ).astype(BF16)
        store(n).start()
    for n in range(parts - 4, parts):
        store(n).wait()


def body(tokens, block_map, slot_keys, gate_weight, up_weight, down_weight):
    _, rows, width = tokens.shape
    slots = slot_keys.shape[1]
    nseq = lax.axis_size("seq")
    ngrp = lax.axis_size("grp")
    hidden = gate_weight.shape[2]
    cw = width // CHUNKS
    bw = cw // 2
    pw = bw // SIDE
    prow = slots // 4
    per = prow // ngrp
    anywhere = pl.BlockSpec(memory_space=pltpu.HBM)
    on_chip = pl.BlockSpec(memory_space=pltpu.VMEM)
    streams = (2, 2, CHUNKS)
    dma = pltpu.SemaphoreType.DMA
    mix, seq_slots = pl.pallas_call(
        functools.partial(layer_kernel, (nseq, ngrp, 3 * slots // 4)),
        out_shape=(
            pltpu.VMEM((rows, slots), BF16),
            pltpu.VMEM((ngrp // 2, 2, 2, 2, per, width), BF16),
        ),
        in_specs=[anywhere] * 6,
        out_specs=(on_chip, on_chip),
        scratch_shapes=[
            pltpu.VMEM((rows, width), BF16),
            pltpu.SMEM(block_map.shape, jnp.int32),
            pltpu.VMEM(slot_keys.shape, BF16),
            pltpu.VMEM(gate_weight.shape, BF16),
            pltpu.VMEM(up_weight.shape, BF16),
            pltpu.VMEM(down_weight.shape, BF16),
            pltpu.VMEM((rows, slots), F32),
            pltpu.VMEM((slots, rows), BF16),
            pltpu.VMEM((slots, BLOCK), F32),
            pltpu.VMEM((2, SIDE, prow, BLOCK), F32),
            pltpu.VMEM((nseq, 2, slots), F32),
            pltpu.VMEM((2, 2, 2, prow, width), BF16),
            pltpu.VMEM((*streams, SIDE, prow, bw), BF16),
            pltpu.VMEM((*streams, ngrp // 2, 2, per, bw), BF16),
            pltpu.VMEM((*streams, SIDE * 2, ngrp // 2, per, pw), BF16),
            pltpu.VMEM((2, CHUNKS, ngrp // 2, 2 * per, pw), BF16),
            pltpu.VMEM((2, CHUNKS, ngrp // 2, 2, per, pw), BF16),
            pltpu.VMEM((2 * CHUNKS, SIDE * ngrp // 2, 2 * per, pw), BF16),
            pltpu.VMEM((2, 2, prow, width), BF16),
            pltpu.VMEM((2, 2 * prow, hidden), F32),
            pltpu.VMEM((2, 2 * prow, hidden), F32),
            pltpu.VMEM((2, CHUNKS, ngrp // 2, 2, per, bw), BF16),
            dma((4,)),
            dma((5,)),
            dma((2, CHUNKS)),
            dma((5, 2)),
            dma,
            dma(streams),
            dma(streams),
            dma(streams),
            dma(streams),
            dma(streams),
        ],
        compiler_params=pltpu.CompilerParams(
            collective_id=0, has_side_effects=True, vmem_limit_bytes=56 << 20
        ),
    )(
        *(
            pltpu.with_memory_space_constraint(x, pltpu.HBM)
            for x in (tokens, block_map, slot_keys, gate_weight, up_weight, down_weight)
        )
    )

    tile = width // 6
    out = pl.pallas_call(
        mix_kernel,
        out_shape=jax.ShapeDtypeStruct((rows, width), BF16),
        in_specs=[on_chip] * 2,
        out_specs=anywhere,
        scratch_shapes=[pltpu.VMEM((4, rows, tile), BF16), dma((4,))],
        compiler_params=pltpu.CompilerParams(vmem_limit_bytes=32 << 20),
    )(mix, seq_slots.reshape(slots, width))
    return out[None]


def solution(mesh):
    placed = (
        P("grp", "seq", None),
        P("grp", "seq"),
        P(),
        P("grp", None, "seq"),
        P("grp", None, "seq"),
        P("grp", "seq", None),
    )
    return jax.shard_map(
        body, mesh=mesh, in_specs=placed, out_specs=P("grp", "seq", None), check_vma=False
    )
```

```python
import functools
import jax
import jax.numpy as jnp
from jax import lax
from jax.experimental import pallas as pl
from jax.experimental.pallas import tpu as pltpu
from jax.sharding import PartitionSpec as P

BLOCK = 128
SIDE = 4
CHUNKS = 3
MESH = pl.DeviceIdType.MESH
F32 = jnp.float32
BF16 = jnp.bfloat16


def loop(start, stop, fn):
    def step(k, carry):
        fn(k)
        return carry

    lax.fori_loop(start, stop, step, 0)


def far_first(n, m):
    def hops(k):
        return min(k // m, n - k // m) + min(k % m, m - k % m)

    return sorted(range(1, n * m), key=hops, reverse=True)


def layer_kernel(
    dims,
    tok_hbm,
    bm_hbm,
    keys_hbm,
    wg_hbm,
    wu_hbm,
    wd_hbm,
    mix_out,
    slots_out,
    tok,
    bm,
    keys,
    wg,
    wu,
    wd,
    logits,
    wts,
    fac,
    scales,
    stat,
    terms,
    first,
    middle,
    second,
    piece_x,
    piece_y,
    counts,
    xs,
    gates,
    ups,
    ys,
    tok_sem,
    in_sem,
    own_sem,
    sent,
    stat_r,
    sum_hr,
    sum_lr,
    put_lr,
    put_hr,
    pass_hr,
):
    nseq, ngrp, image_slots = dims
    me = lax.axis_index("seq")
    grp = lax.axis_index("grp")
    level, core = grp // 2, lax.rem(grp, 2)
    levels = ngrp // 2
    rows, width = tok.shape
    slots = keys.shape[1]
    tchunk = rows // 4
    blocks = rows // BLOCK
    cw = width // CHUNKS
    bw = cw // 2
    pw = bw // SIDE
    prow = slots // 4
    per_grp = prow // ngrp
    at_x, at_y = me // SIDE, lax.rem(me, SIDE)
    place = ((at_x, at_y), (at_y, at_x))

    def seq_of(h, u, v):
        return u * SIDE + v if h == 0 else v * SIDE + u

    def block_cols(s, u):
        return pl.ds(pl.multiple_of(s * cw + lax.rem(u, 2) * bw, bw), bw)

    def piece_cols(s, u, v):
        return pl.ds(pl.multiple_of(s * cw + lax.rem(u, 2) * bw + v * pw, pw), pw)

    def piece_at(v):
        return pl.ds(pl.multiple_of(v * pw, pw), pw)

    bm_copy = pltpu.make_async_copy(bm_hbm, bm, in_sem.at[4])
    bm_copy.start()
    keys_copy = pltpu.make_async_copy(keys_hbm, keys, in_sem.at[0])
    keys_copy.start()

    def tok_copy(r):
        at = pl.ds(pl.multiple_of(r * tchunk, tchunk), tchunk)
        return pltpu.make_async_copy(tok_hbm.at[0, at], tok.at[at], tok_sem.at[r])

    tok_copy(0).start()
    wg_copy = pltpu.make_async_copy(wg_hbm, wg, in_sem.at[1])
    wu_copy = pltpu.make_async_copy(wu_hbm, wu, in_sem.at[2])
    wd_copy = pltpu.make_async_copy(wd_hbm, wd, in_sem.at[3])

    barrier = pltpu.get_barrier_semaphore()

    def greet(peer):
        pl.semaphore_signal(barrier, inc=1, device_id=peer, device_id_type=MESH)

    for h in range(2):
        u, v = place[h]

        def greet_line(k):
            peer = seq_of(h, u, lax.rem(v + k, SIDE))
            greet({"seq": peer, "grp": level * 2 + 1 - core})

            def greet_level(n):
                greet({"seq": peer, "grp": lax.rem(level + n, levels) * 2 + core})

            loop(1, levels, greet_level)

        def greet_near(k):
            greet({"seq": seq_of(h, u, lax.rem(v + k, SIDE))})

        loop(h, SIDE, greet_line)
        loop(1, SIDE, greet_near)

    def greet_rest(k):
        x = lax.rem(at_x + 1 + k // (SIDE - 1), SIDE)
        y = lax.rem(at_y + 1 + lax.rem(k, SIDE - 1), SIDE)
        greet({"seq": x * SIDE + y})

    loop(0, (SIDE - 1) * (SIDE - 1), greet_rest)
    loop(1, 4, lambda r: tok_copy(r).start())
    greeted = (2 * SIDE - 1) * levels + nseq - 1

    def to(src, dst, ssem, rsem, peer, **more):
        return pltpu.make_async_remote_copy(
            src_ref=src,
            dst_ref=dst,
            send_sem=ssem,
            recv_sem=rsem,
            device_id={"seq": peer, **more},
            device_id_type=MESH,
        )

    text_lane = (lax.broadcasted_iota(jnp.int32, (1, slots), 1) >= image_slots).astype(jnp.int32)

    def by_stream(x):
        wide = slots // 16
        return jnp.concatenate(
            [
                x[(2 * g + h) * 16 + t * 8 : (2 * g + h) * 16 + t * 8 + 8]
                for h in range(2)
                for t in range(2)
                for g in range(wide // 2)
            ],
            axis=0,
        )

    bm_copy.wait()
    keys_copy.wait()
    per = tchunk // BLOCK

    def logit_chunk(r, peak):
        tok_copy(r).wait()
        at = pl.ds(pl.multiple_of(r * tchunk, tchunk), tchunk)
        got = jnp.dot(tok[at], keys[...], preferred_element_type=F32)
        for b in range(per):
            block = jnp.where(
                text_lane == bm[0, r * per + b], got[b * BLOCK : (b + 1) * BLOCK], -1e30
            )
            logits[pl.ds(pl.multiple_of(r * tchunk + b * BLOCK, BLOCK), BLOCK)] = block
            peak = jnp.maximum(peak, jnp.max(block, axis=0, keepdims=True))
        return peak

    peak = lax.fori_loop(0, 4, logit_chunk, jnp.full((1, slots), -1e30, F32))
    wg_copy.start()
    wu_copy.start()
    wd_copy.start()

    def weigh(b, total):
        at = pl.ds(pl.multiple_of(b * BLOCK, BLOCK), BLOCK)
        w = jnp.where(text_lane == bm[0, b], jnp.exp(logits[at] - peak), 0.0)
        wts[:, at] = by_stream(w.T).astype(BF16)
        return total + jnp.sum(w, axis=0, keepdims=True)

    total = lax.fori_loop(0, blocks, weigh, jnp.zeros((1, slots), F32))
    stat[me, 0:1] = peak
    stat[me, 1:2] = total

    pl.semaphore_wait(barrier, greeted)

    def stat_copy(peer, src):
        return to(stat.at[src], stat.at[src], sent.at[0, 0], stat_r, peer)

    loop(1, nseq, lambda k: stat_copy(lax.rem(me + k, nseq), me).start())

    def around(n, at, k):
        return lax.rem(at + k, n)

    def before(n, at, k):
        return lax.rem(at + n - k, n)

    def sum_heavy(p, h, s, dst, src):
        _, v = place[h]
        return to(
            terms.at[p, h, dst // 2, :, block_cols(s, dst)],
            first.at[p, h, s, src],
            sent.at[1, p],
            sum_hr.at[p, h, s],
            seq_of(h, dst, v),
        )

    def sum_light(p, h, s, dst, dst_core, src, src_core):
        u, _ = place[h]
        return to(
            middle.at[p, h, s, :, dst_core, :, piece_at(dst)],
            second.at[p, h, s, src * 2 + src_core],
            sent.at[2, p],
            sum_lr.at[p, h, s],
            seq_of(h, u, dst),
            grp=level * 2 + dst_core,
        )

    def put_light(p, h, s, dst, dst_level, src, src_level):
        u, _ = place[h]
        if p == 0:
            here = piece_x.at[h, s, dst_level]
            at = pl.ds(pl.multiple_of(src_level * 2 * per_grp, 2 * per_grp), 2 * per_grp)
            there = xs.at[h, u // 2, at, piece_cols(s, u, src)]
        else:
            here = piece_y.at[h, s, dst_level]
            there = ys.at[h, s, src_level, :, :, piece_at(src)]
        return to(
            here,
            there,
            sent.at[3, p],
            put_lr.at[p, h, s],
            seq_of(h, u, dst),
            grp=dst_level * 2 + core,
        )

    def put_heavy(p, h, s, dst, src):
        u, v = place[h]
        if p == 0:
            here = xs.at[h, u // 2, :, block_cols(s, u)]
            there = xs.at[h, src // 2, :, block_cols(s, src)]
        else:
            here = ys.at[h, s]
            there = slots_out.at[:, :, h, src // 2, :, block_cols(s, src)]
        return to(
            here,
            there,
            sent.at[4, p],
            put_hr.at[p, h, s],
            seq_of(h, dst, v),
        )

    def pass_half(p, h, s, side):
        u, v = place[h]
        step = (1, SIDE - 1)[side]
        src, dst = before(SIDE, u, step), around(SIDE, u, step)
        if p == 0:
            rows_of = slice(side * prow // 2, (side + 1) * prow // 2)
            half = xs.at[h, src // 2, rows_of, block_cols(s, src)]
        else:
            levels_of = slice(side * levels // 2, (side + 1) * levels // 2)
            half = slots_out.at[levels_of, :, h, src // 2, :, block_cols(s, src)]
        return to(half, half, sent.at[4, p], pass_hr.at[p, h, s], seq_of(h, dst, v))

    def own_copy(h, s):
        u, _ = place[h]
        return pltpu.make_async_copy(
            ys.at[h, s],
            slots_out.at[:, :, h, u // 2, :, block_cols(s, u)],
            own_sem.at[h, s],
        )

    def start_sum(p, h, s):
        u, _ = place[h]
        loop(1, SIDE, lambda k: sum_heavy(p, h, s, around(SIDE, u, k), u).start())

    def arrived(ref, sem):
        pltpu.make_async_copy(ref, ref, sem).wait()

    def mid_sum(p, h, s):
        u, v = place[h]
        acc = terms[p, h, u // 2, :, block_cols(s, u)].astype(F32)
        arrived(first.at[p, h, s, : SIDE - 1], sum_hr.at[p, h, s])
        if p == 0:
            acc = acc * scale_of(h, 0)
        for k in range(1, SIDE):
            got = first[p, h, s, before(SIDE, u, k)].astype(F32)
            acc = acc + (got if p else got * scale_of(h, k))
        middle[p, h, s] = acc.reshape(middle.shape[3:]).astype(BF16)

        def send(k):
            dst, dst_core = around(SIDE, v, k // 2), lax.rem(core + k, 2)
            sum_light(p, h, s, dst, dst_core, v, core).start()

        for k in far_first(SIDE, 2):
            send(k)
        second[p, h, s, v * 2 + core] = middle[p, h, s, :, core, :, piece_at(v)]

    def scale_of(h, k):
        return jnp.concatenate([scales[h, k]] * (bw // BLOCK), axis=1)

    def end_sum(p, h, s):
        u, v = place[h]
        arrived(second.at[p, h, s, : SIDE * 2 - 1], sum_lr.at[p, h, s])
        for c in range(2):
            acc = second[p, h, s, c].astype(F32)
            for k in range(1, SIDE):
                acc = acc + second[p, h, s, 2 * k + c].astype(F32)
            if p == 0:
                piece_x[h, s, :, c * per_grp : (c + 1) * per_grp] = acc.astype(BF16)
            else:
                piece_y[h, s, :, c] = acc.astype(BF16)

        def send(k):
            dst, dst_level = around(SIDE, v, k // levels), around(levels, level, lax.rem(k, levels))
            put_light(p, h, s, dst, dst_level, v, level).start()

        for k in far_first(SIDE, levels):
            send(k)
        if p == 0:
            at = pl.ds(pl.multiple_of(level * 2 * per_grp, 2 * per_grp), 2 * per_grp)
            xs[h, u // 2, at, piece_cols(s, u, v)] = piece_x[h, s, level]
        else:
            ys[h, s, level, :, :, piece_at(v)] = piece_y[h, s, level]

    def mid_put(p, h, s):
        u, v = place[h]
        arrived(counts.at[0, : SIDE * levels - 1], put_lr.at[p, h, s])
        u, _ = place[h]
        for k in (1, 2, 3) if s >= 1 else (1, 3):
            put_heavy(p, h, s, around(SIDE, u, k), u).start()
        if p == 1:
            own_copy(h, s).start()

    def pass_put(p, h, s):
        arrived(first.at[p, h, s, :2], put_hr.at[p, h, s])
        for side in range(2):
            pass_half(p, h, s, side).start()

    def end_put(p, h, s):
        if s < 1:
            arrived(first.at[p, h, s, 0], pass_hr.at[p, h, s])
        else:
            arrived(first.at[p, h, s, : SIDE - 1], put_hr.at[p, h, s])
        if p == 1:
            own_copy(h, s).wait()
            return
        x = xs[h, :, :, s * cw : (s + 1) * cw].reshape(2 * prow, cw)
        gate = jnp.dot(x, wg[h, s * cw : (s + 1) * cw], preferred_element_type=F32)
        up = jnp.dot(x, wu[h, s * cw : (s + 1) * cw], preferred_element_type=F32)
        if s > 0:
            gate = gate + gates[h]
            up = up + ups[h]
        if s < CHUNKS - 1:
            gates[h] = gate
            ups[h] = up
            return
        gates[h] = gate / (1.0 + jnp.exp(-gate)) * up
        if h == 0:
            return
        for n in range(CHUNKS):
            for e in range(2):
                at = slice(n * cw, (n + 1) * cw)
                out = jnp.dot(gates[e].astype(BF16), wd[e, :, at], preferred_element_type=F32)
                terms[1, e, :, :, at] = out.reshape(2, prow, cw).astype(BF16)
                if n < 2:
                    start_sum(1, e, n)

    def mix_rows(b):
        at = pl.ds(pl.multiple_of(b * BLOCK, BLOCK), BLOCK)
        m = logits[at]
        e = jnp.where(text_lane == bm[0, b], jnp.exp(m - jnp.max(m, axis=1, keepdims=True)), 0.0)
        mix_out[at] = (e / jnp.sum(e, axis=1, keepdims=True)).astype(BF16)

    for s in range(CHUNKS):
        at = slice(s * cw, (s + 1) * cw)
        out = jnp.dot(wts[...], tok[:, at], preferred_element_type=F32)
        terms[0, :, :, :, at] = out.reshape(2, 2, prow, cw).astype(BF16)
        if s < 2:
            for h in range(2):
                start_sum(0, h, s)

    loop(0, blocks, mix_rows)
    arrived(stat.at[: nseq - 1], stat_r)
    peaks = stat[:, 0, :]
    top = jnp.max(peaks, axis=0, keepdims=True)
    whole = jnp.sum(jnp.exp(peaks - top) * stat[:, 1, :], axis=0, keepdims=True)
    near = []
    for h in range(2):
        u, v = place[h]
        for k in range(SIDE):
            near.append(stat[seq_of(h, before(SIDE, u, k), v), 0:1])
    near = jnp.exp(jnp.concatenate(near, axis=0) - top) / whole
    fac[...] = by_stream(jnp.concatenate([near] * (BLOCK // (2 * SIDE)), axis=0).T)
    for h in range(2):
        u, _ = place[h]
        mine = fac[pl.ds(pl.multiple_of(h * 2 * prow + (u // 2) * prow, prow), prow)]
        for k in range(SIDE):
            scales[h, k] = jnp.broadcast_to(
                mine[:, h * SIDE + k : h * SIDE + k + 1], (prow, BLOCK)
            )

    order = (
        (mid_sum, 0),
        (start_sum, 2),
        (mid_sum, 1),
        (end_sum, 0),
        (mid_sum, 2),
        (end_sum, 1),
        (mid_put, 0),
        (end_sum, 2),
        (mid_put, 1),
        (pass_put, 0),
        (mid_put, 2),
        (end_put, 0),
        (end_put, 1),
        (end_put, 2),
    )

    for p in range(2):
        for step, s in order:
            if p == 0 and (step, s) == (end_put, 0):
                wg_copy.wait()
                wu_copy.wait()
                wd_copy.wait()
            for h in range(2):
                step(p, h, s)


    arrived(stat.at[: nseq - 1], sent.at[0, 0])
    for p in range(2):
        arrived(first.at[p, :, :, : SIDE - 1], sent.at[1, p])
        arrived(second.at[p, :, :, : SIDE * 2 - 1], sent.at[2, p])
        arrived(counts.at[:, : SIDE * levels - 1], sent.at[3, p])
        arrived(first.at[p, :, :, : SIDE - 1], sent.at[4, p])


def mix_kernel(mix, slots, out_hbm, out, out_sem):
    tile = out.shape[2]
    parts = slots.shape[1] // tile

    def store(n):
        at = slice(n * tile, (n + 1) * tile)
        return pltpu.make_async_copy(out.at[n % 4], out_hbm.at[:, at], out_sem.at[n % 4])

    for n in range(parts):
        if n >= 4:
            store(n - 4).wait()
        out[n % 4] = jnp.dot(
            mix[...], slots[:, n * tile : (n + 1) * tile], preferred_element_type=F32
        ).astype(BF16)
        store(n).start()
    for n in range(parts - 4, parts):
        store(n).wait()


def body(tokens, block_map, slot_keys, gate_weight, up_weight, down_weight):
    _, rows, width = tokens.shape
    slots = slot_keys.shape[1]
    nseq = lax.axis_size("seq")
    ngrp = lax.axis_size("grp")
    hidden = gate_weight.shape[2]
    cw = width // CHUNKS
    bw = cw // 2
    pw = bw // SIDE
    prow = slots // 4
    per = prow // ngrp
    anywhere = pl.BlockSpec(memory_space=pltpu.HBM)
    on_chip = pl.BlockSpec(memory_space=pltpu.VMEM)
    streams = (2, 2, CHUNKS)
    dma = pltpu.SemaphoreType.DMA
    mix, seq_slots = pl.pallas_call(
        functools.partial(layer_kernel, (nseq, ngrp, 3 * slots // 4)),
        out_shape=(
            pltpu.VMEM((rows, slots), BF16),
            pltpu.VMEM((ngrp // 2, 2, 2, 2, per, width), BF16),
        ),
        in_specs=[anywhere] * 6,
        out_specs=(on_chip, on_chip),
        scratch_shapes=[
            pltpu.VMEM((rows, width), BF16),
            pltpu.SMEM(block_map.shape, jnp.int32),
            pltpu.VMEM(slot_keys.shape, BF16),
            pltpu.VMEM(gate_weight.shape, BF16),
            pltpu.VMEM(up_weight.shape, BF16),
            pltpu.VMEM(down_weight.shape, BF16),
            pltpu.VMEM((rows, slots), F32),
            pltpu.VMEM((slots, rows), BF16),
            pltpu.VMEM((slots, BLOCK), F32),
            pltpu.VMEM((2, SIDE, prow, BLOCK), F32),
            pltpu.VMEM((nseq, 2, slots), F32),
            pltpu.VMEM((2, 2, 2, prow, width), BF16),
            pltpu.VMEM((*streams, SIDE, prow, bw), BF16),
            pltpu.VMEM((*streams, ngrp // 2, 2, per, bw), BF16),
            pltpu.VMEM((*streams, SIDE * 2, ngrp // 2, per, pw), BF16),
            pltpu.VMEM((2, CHUNKS, ngrp // 2, 2 * per, pw), BF16),
            pltpu.VMEM((2, CHUNKS, ngrp // 2, 2, per, pw), BF16),
            pltpu.VMEM((2 * CHUNKS, SIDE * ngrp // 2, 2 * per, pw), BF16),
            pltpu.VMEM((2, 2, prow, width), BF16),
            pltpu.VMEM((2, 2 * prow, hidden), F32),
            pltpu.VMEM((2, 2 * prow, hidden), F32),
            pltpu.VMEM((2, CHUNKS, ngrp // 2, 2, per, bw), BF16),
            dma((4,)),
            dma((5,)),
            dma((2, CHUNKS)),
            dma((5, 2)),
            dma,
            dma(streams),
            dma(streams),
            dma(streams),
            dma(streams),
            dma(streams),
        ],
        compiler_params=pltpu.CompilerParams(
            collective_id=0, has_side_effects=True, vmem_limit_bytes=56 << 20
        ),
    )(
        *(
            pltpu.with_memory_space_constraint(x, pltpu.HBM)
            for x in (tokens, block_map, slot_keys, gate_weight, up_weight, down_weight)
        )
    )

    tile = width // 6
    out = pl.pallas_call(
        mix_kernel,
        out_shape=jax.ShapeDtypeStruct((rows, width), BF16),
        in_specs=[on_chip] * 2,
        out_specs=anywhere,
        scratch_shapes=[pltpu.VMEM((4, rows, tile), BF16), dma((4,))],
        compiler_params=pltpu.CompilerParams(vmem_limit_bytes=32 << 20),
    )(mix, seq_slots.reshape(slots, width))
    return out[None]


def solution(mesh):
    placed = (
        P("grp", "seq", None),
        P("grp", "seq"),
        P(),
        P("grp", None, "seq"),
        P("grp", None, "seq"),
        P("grp", "seq", None),
    )
    return jax.shard_map(
        body, mesh=mesh, in_specs=placed, out_specs=P("grp", "seq", None), check_vma=False
    )
```
